32 devices in a mesh: seq: 4 (over x, core), dp: 8 (over z, y).
Axes of the slice: x: 2, y: 2, z: 4, core: 2. Of those that a mesh axis runs over, the one named last changes fastest.
Arguments:
- inputs: bfloat16 [8, 1024, 4096], P('dp', 'seq'), may hold values from -6 to 6
- queries: bfloat16 [8, 1024, 256], P('dp', 'seq'), may hold values from -6 to 6
- keys: bfloat16 [8, 1024, 256], P('dp', 'seq'), may hold values from -6 to 6
- values: bfloat16 [8, 1024, 256], P('dp', 'seq'), may hold values from -6 to 6
- out_grad: bfloat16 [8, 1024, 256], P('dp', 'seq'), may hold values from -6 to 6
Outputs:
- qkv_grad: bfloat16 [8, 1024, 768], P('dp', 'seq')
- weight_grad: float32 [4096, 768], P('dp')
The draws below stay inside these ranges and needn't reach their ends.
All inputs are finite; a program needn't handle non-finite values.
Results may differ from the reference program's by a relative error of at most 0.014.
Values may be sent and summed in bfloat16 or wider, within the bound.
No kernel may reach another device: no remote copies, remote signals or barrier semaphores. Data moves between devices by JAX's collectives and lax.ppermute only.
A program may use at most 64 MiB of HBM per device.

```python
import jax
import jax.numpy as jnp
from jax import lax

D = 4096
HS = 128
HEADS = 2
L_DEV = 256
HW = 256
LENGTH = 1024
BATCH = 8
N_SEQ = 4


def raised(values, stream_key, source, target, shards_of, factor):
    owner, partner = [(jnp.arange(values.shape[position]) // (values.shape[position] // shards_of)).reshape([-1 if axis == position else 1 for axis in range(values.ndim)]) for position in (source, target)]
    chosen = jax.random.permutation(stream_key, shards_of)[partner]
    strong = (owner == chosen) | (owner == (partner + shards_of // 2) % shards_of)
    return jnp.where(strong, factor * values, values)


def steps_of(stream_key, extent, cuts, smallest, high):
    loudness = 1.0
    for position, blocks in cuts:
        draws = jax.random.uniform(jax.random.fold_in(jax.random.fold_in(stream_key, 6), position), (blocks,), jnp.float32, smallest / len(cuts), high / len(cuts))
        loudness = loudness * jnp.repeat(jnp.exp(draws), extent[position] // blocks).reshape((-1,) + (1,) * (len(extent) - 1 - position))
    return loudness


def bell_draw(stream_key, shape, spread, reach, cuts=(), held_as=jnp.bfloat16):
    loudness = steps_of(stream_key, shape, cuts, -0.22, 0.18) if cuts else 1.0
    result = jax.random.normal(stream_key, shape, jnp.float32) * spread * loudness
    return jnp.minimum(jnp.maximum(result, -reach), reach).astype(held_as)


def heavy_noise(own_key, dims, deviation, bound, shards, heavy, kind=jnp.bfloat16):
    array = deviation * jax.random.normal(own_key, dims, jnp.float32)
    if shards:
        array = array * steps_of(own_key, dims, shards, -0.22, 0.18)
    return jnp.clip(raised(array, jax.random.fold_in(own_key, 3), *heavy), -bound, bound).astype(kind)


def setup_inputs(seed: int = 0) -> dict:
    key_list = jax.random.split(jax.random.key(seed), 6)
    inputs = heavy_noise(key_list[0], (BATCH, LENGTH, D), 1.0, 6.0, ((0, 8), (1, 4)), (0, 2, 8, 2.0))
    queries = bell_draw(key_list[1], (BATCH, LENGTH, HW), 1.0, 6.0, ((0, 8), (1, 4)))
    keys = bell_draw(key_list[2], (BATCH, LENGTH, HW), 1.0, 6.0, ((0, 8), (1, 4)))
    values = bell_draw(key_list[3], (BATCH, LENGTH, HW), 1.0, 6.0, ((0, 8), (1, 4)))
    out_grad = bell_draw(key_list[4], (BATCH, LENGTH, HW), 1.0, 6.0, ((0, 8), (1, 4)))
    return dict(inputs=inputs, queries=queries, keys=keys, values=values, out_grad=out_grad)


def block_grads(query, key, value, grad_out, prefix, suffix, scale):
    query = query.astype(jnp.float32)
    key = key.astype(jnp.float32)
    value = value.astype(jnp.float32)
    grad_out = grad_out.astype(jnp.float32)
    prefix = prefix.astype(jnp.float32)
    suffix = suffix.astype(jnp.float32)
    count = query.shape[0]
    causal = jnp.arange(count)[:, None] >= jnp.arange(count)[None, :]
    score_a = jnp.einsum('thd,shd->hts', grad_out, value)
    score_a = jnp.where(causal[None], score_a, 0.0).astype(jnp.bfloat16).astype(jnp.float32)
    score_b = jnp.einsum('thd,shd->hts', query, key)
    score_b = jnp.where(causal[None], score_b, 0.0).astype(jnp.bfloat16).astype(jnp.float32)
    grad_q = jnp.einsum('hts,shd->thd', score_a, key) + jnp.einsum('thb,hab->tha', grad_out, prefix)
    grad_k = jnp.einsum('htj,thd->jhd', score_a, query) + jnp.einsum('jhb,hab->jha', value, suffix)
    grad_v = jnp.einsum('htj,thd->jhd', score_b, grad_out) + jnp.einsum('jha,hab->jhb', key, suffix)
    joined = jnp.concatenate([grad_q, grad_k, grad_v], axis=1) * scale
    return joined.reshape(count, -1).astype(jnp.bfloat16)

def reference(inputs, queries, keys, values, out_grad):
    scale = 1.0 / jnp.sqrt(jnp.float32(HS * LENGTH))
    weight_scale = 1.0 / jnp.sqrt(jnp.float32(BATCH * LENGTH))
    shape = (BATCH * N_SEQ, L_DEV, HEADS, HS)
    query = queries.reshape(shape)
    key = keys.reshape(shape)
    value = values.reshape(shape)
    grad_out = out_grad.reshape(shape)
    kv_state = jnp.einsum('nlhi,nlhj->nhij', key.astype(jnp.float32), value.astype(jnp.float32)).astype(jnp.bfloat16)
    dq_state = jnp.einsum('nlhi,nlhj->nhij', query.astype(jnp.float32), grad_out.astype(jnp.float32)).astype(jnp.bfloat16)
    kv_wide = lax.optimization_barrier(kv_state).astype(jnp.float32).reshape(BATCH, N_SEQ, HEADS, HS, HS)
    dq_wide = lax.optimization_barrier(dq_state).astype(jnp.float32).reshape(BATCH, N_SEQ, HEADS, HS, HS)
    zeros = jnp.zeros((BATCH, 1, HEADS, HS, HS), jnp.float32)
    prefix = jnp.concatenate([zeros, jnp.cumsum(kv_wide, axis=1)[:, :-1]], axis=1)
    suffix_rev = jnp.cumsum(dq_wide[:, ::-1], axis=1)
    suffix = jnp.concatenate([suffix_rev[:, :-1][:, ::-1], zeros], axis=1)
    prefix = prefix.astype(jnp.bfloat16).reshape(BATCH * N_SEQ, HEADS, HS, HS)
    suffix = suffix.astype(jnp.bfloat16).reshape(BATCH * N_SEQ, HEADS, HS, HS)
    flat_inputs = inputs.reshape(BATCH * N_SEQ, L_DEV, D)

    def step(total, pieces):
        q_b, k_b, v_b, g_b, p_b, s_b, x_b = pieces
        grads = block_grads(q_b, k_b, v_b, g_b, p_b, s_b, scale)
        partial_value = lax.dot_general(x_b, grads, (((0,), (0,)), ((), ())), preferred_element_type=jnp.float32) * weight_scale
        partial_value = partial_value.astype(jnp.bfloat16).astype(jnp.float32)
        return (total + partial_value, grads)
    start = jnp.zeros((D, 3 * HW), jnp.float32)
    weight_grad, grads = lax.scan(step, start, (query, key, value, grad_out, prefix, suffix, flat_inputs))
    qkv_grad = grads.reshape(BATCH, LENGTH, 3 * HW)
    return (qkv_grad, weight_grad)
```

```python
import functools

import jax
import jax.numpy as jnp
from jax import lax
from jax.experimental import pallas as pl
from jax.experimental.pallas import tpu as pltpu
from jax.sharding import PartitionSpec as P

HS = 128
HEADS = 2
BLOCK = 128
BF16 = jnp.bfloat16
F32 = jnp.float32
AXES = ("seq", "dp")


def block_grads(query, key, value, grad_out, prefix, suffix, scale):
    count = query.shape[0]
    causal = jnp.arange(count)[:, None] >= jnp.arange(count)[None, :]
    f32 = jnp.float32
    score_a = jnp.einsum("thd,shd->hts", grad_out, value, preferred_element_type=f32)
    score_a = jnp.where(causal[None], score_a, 0.0).astype(jnp.bfloat16)
    score_b = jnp.einsum("thd,shd->hts", query, key, preferred_element_type=f32)
    score_b = jnp.where(causal[None], score_b, 0.0).astype(jnp.bfloat16)
    grad_q = jnp.einsum("hts,shd->thd", score_a, key, preferred_element_type=f32) + jnp.einsum(
        "thb,hab->tha", grad_out, prefix, preferred_element_type=f32
    )
    grad_k = jnp.einsum("htj,thd->jhd", score_a, query, preferred_element_type=f32) + jnp.einsum(
        "jhb,hab->jha", value, suffix, preferred_element_type=f32
    )
    grad_v = jnp.einsum("htj,thd->jhd", score_b, grad_out, preferred_element_type=f32) + jnp.einsum(
        "jha,hab->jhb", key, suffix, preferred_element_type=f32
    )
    joined = jnp.concatenate([grad_q, grad_k, grad_v], axis=1) * scale
    return joined.reshape(count, -1).astype(jnp.bfloat16)


def on_device_any(inputs, queries, keys, values, out_grad):
    tokens = queries.shape[1]
    seq_count = lax.axis_size("seq")
    batch_count = lax.axis_size("dp")
    length_all = tokens * seq_count
    scale = 1.0 / jnp.sqrt(jnp.float32(HS * length_all))
    weight_scale = 1.0 / jnp.sqrt(jnp.float32(batch_count * length_all))
    shape = (tokens, HEADS, HS)
    query = queries[0].reshape(shape)
    key = keys[0].reshape(shape)
    value = values[0].reshape(shape)
    grad_out = out_grad[0].reshape(shape)
    kv_state = jnp.einsum("lhi,lhj->hij", key, value, preferred_element_type=jnp.float32).astype(
        jnp.bfloat16
    )
    dq_state = jnp.einsum(
        "lhi,lhj->hij", query, grad_out, preferred_element_type=jnp.float32
    ).astype(jnp.bfloat16)
    stacked = jnp.stack([kv_state, dq_state])[None]
    position = lax.axis_index("seq")
    piece = lax.all_gather(stacked, "seq", axis=0, tiled=True)
    owners = jnp.arange(piece.shape[0])
    lower = (owners < position).astype(jnp.float32)
    higher = (owners > position).astype(jnp.float32)
    wide = piece.astype(jnp.float32)
    prefix = jnp.einsum("n,nhij->hij", lower, wide[:, 0])
    suffix = jnp.einsum("n,nhij->hij", higher, wide[:, 1])
    prefix = prefix.astype(jnp.bfloat16)
    suffix = suffix.astype(jnp.bfloat16)
    grads = block_grads(query, key, value, grad_out, prefix, suffix, scale)
    features = inputs[0]
    rows_here = lax.psum_scatter(
        (
            lax.dot_general(
                features, grads, (((0,), (0,)), ((), ())), preferred_element_type=jnp.float32
            )
            * weight_scale
        ).astype(jnp.bfloat16),
        "dp",
        scatter_dimension=0,
        tiled=True,
    )
    weight_grad = lax.psum(rows_here, "seq").astype(jnp.float32)
    return (grads[None], weight_grad)


def dot(a, b, a_dim, b_dim):
    return lax.dot_general(a, b, (((a_dim,), (b_dim,)), ((), ())), preferred_element_type=F32)


def head(ref, h):
    return ref[:, h * HS : (h + 1) * HS]


def vmem():
    return pl.BlockSpec(memory_space=pltpu.VMEM)


def smem():
    return pl.BlockSpec(memory_space=pltpu.SMEM)


def state_kernel(meta, q, k, v, g, send, packed):
    upper = meta[1] == 1
    for h in range(HEADS):
        left = jnp.where(upper, head(q, h), head(k, h))
        right = jnp.where(upper, head(g, h), head(v, h))
        send[h] = dot(left, right, 0, 0).astype(BF16)
    for i, ref in enumerate((q, k, v, g)):
        packed[i] = ref[...]


def local_kernel(q, k, v, g, other, local, states):
    count = q.shape[0]
    row = lax.broadcasted_iota(jnp.int32, (count, count), 0)
    causal = row >= lax.broadcasted_iota(jnp.int32, (count, count), 1)
    for b, block in enumerate(((q, k, v, g), tuple(other.at[i] for i in range(4)))):
        for h in range(HEADS):
            qh, kh, vh, gh = (head(ref, h) for ref in block)
            score_a = jnp.where(causal, dot(gh, vh, 1, 1), 0.0).astype(BF16)
            score_b = jnp.where(causal, dot(qh, kh, 1, 1), 0.0).astype(BF16)
            local[b, 0, :, h * HS : (h + 1) * HS] = dot(score_a, kh, 1, 0)
            local[b, 1, :, h * HS : (h + 1) * HS] = dot(score_a, qh, 0, 0)
            local[b, 2, :, h * HS : (h + 1) * HS] = dot(score_b, gh, 0, 0)
            states[b, 0, h] = dot(kh, vh, 0, 0).astype(BF16)
            states[b, 1, h] = dot(qh, gh, 0, 0).astype(BF16)


def grads_kernel(meta, k, v, g, other, local, states, near, far, grads, *, scale):
    core = meta[0].astype(F32)
    upper = meta[1].astype(F32)
    width = HEADS * HS
    for h in range(HEADS):
        outside = near[h].astype(F32) + far[h].astype(F32)
        before = outside * upper
        after = outside * (1.0 - upper)
        for b, (kb, vb, gb) in enumerate(((k, v, g), (other.at[1], other.at[2], other.at[3]))):
            late = core if b == 0 else 1.0 - core
            prefix = (before + states[1 - b, 0, h].astype(F32) * late).astype(BF16)
            suffix = (after + states[1 - b, 1, h].astype(F32) * (1.0 - late)).astype(BF16)
            cols = slice(h * HS, (h + 1) * HS)
            extra = (
                dot(head(gb, h), prefix, 1, 1),
                dot(head(vb, h), suffix, 1, 1),
                dot(head(kb, h), suffix, 1, 0),
            )
            for part in range(3):
                total = (local[b, part, :, cols] + extra[part]) * scale
                grads[b, :, part * width + h * HS : part * width + (h + 1) * HS] = total.astype(BF16)


def weight_kernel(meta, x, other, grads, out, *, scale):
    total = dot(x[...], grads[0], 0, 0) + dot(other[...], grads[1], 0, 0)
    out[0] = (total * scale).astype(BF16)


def weight_part(meta, features, other, grads, first, blocks, scale):
    tokens, width = features.shape
    column = lambda i, table: (0, table[4 + first + i])
    return pl.pallas_call(
        functools.partial(weight_kernel, scale=scale),
        grid_spec=pltpu.PrefetchScalarGridSpec(
            num_scalar_prefetch=1,
            grid=(blocks,),
            in_specs=[
                pl.BlockSpec((tokens, BLOCK), column),
                pl.BlockSpec((tokens, BLOCK), column),
                pl.BlockSpec(grads.shape, lambda i, table: (0, 0, 0)),
            ],
            out_specs=pl.BlockSpec((1, BLOCK, grads.shape[2]), lambda i, table: (i, 0, 0)),
        ),
        out_shape=jax.ShapeDtypeStruct((blocks, BLOCK, grads.shape[2]), BF16),
        cost_estimate=pl.CostEstimate(
            flops=4 * tokens * BLOCK * blocks * grads.shape[2],
            bytes_accessed=4 * tokens * BLOCK * blocks + 2 * blocks * BLOCK * grads.shape[2],
            transcendentals=0,
        ),
    )(meta, features, other, grads)


def place_kernel(meta, own, near, pair, out):
    mine = meta[2]
    for turn, block in ((0, own[...]), (2, near[...]), (1, pair[0]), (3, pair[1])):
        start = pl.multiple_of((mine ^ turn) * BLOCK, BLOCK)
        out[pl.ds(start, BLOCK), :] = block.astype(F32)


def partners(core0, core1, seq_count, dp_count):
    pairs = []
    for s in range(seq_count):
        for d in range(dp_count):
            ds, dd = (core0, core1)[s % 2]
            pairs.append((s * dp_count + d, (s ^ ds) * dp_count + (d ^ dd)))
    return pairs


def on_device(inputs, queries, keys, values, out_grad):
    tokens = queries.shape[1]
    seq_count = lax.axis_size("seq")
    dp_count = lax.axis_size("dp")
    length_all = tokens * seq_count
    scale = float(1.0 / (HS * length_all) ** 0.5)
    weight_scale = float(1.0 / (dp_count * length_all) ** 0.5)
    features, q, k, v, g = inputs[0], queries[0], keys[0], values[0], out_grad[0]
    width = q.shape[1]
    rows = features.shape[1] // (seq_count * dp_count)

    swap = lambda value, core0, core1: lax.ppermute(
        value, AXES, partners(core0, core1, seq_count, dp_count)
    )
    sibling, across, y, z1, z2 = (1, 0), (2, 0), (0, 1), (0, 2), (0, 4)

    s, d = lax.axis_index("seq"), lax.axis_index("dp")
    core, upper = s & 1, s >> 1
    lane = jnp.arange(20, dtype=jnp.int32)
    bits = lane - 4
    b1, b2, b3, b4 = (bits >> 3) & 1, (bits >> 2) & 1, (bits >> 1) & 1, bits & 1
    row_s = s ^ (2 * jnp.where(core == 0, b1, b2))
    row_d = d ^ jnp.where(core == 0, b2 * 1, b1 * 1) ^ (2 * b3) ^ (4 * b4)
    place = row_d * seq_count + row_s
    meta = jnp.where(
        lane == 0, core, jnp.where(lane == 1, upper, jnp.where(lane == 2, s, place))
    ).astype(jnp.int32)

    send, packed = pl.pallas_call(
        state_kernel,
        in_specs=[smem()] + [vmem()] * 4,
        out_specs=[vmem()] * 2,
        out_shape=[
            jax.ShapeDtypeStruct((HEADS, HS, HS), BF16),
            jax.ShapeDtypeStruct((4, tokens, width), BF16),
        ],
    )(meta, q, k, v, g)
    near = swap(send, across, across)
    far = swap(send, (3, 0), (3, 0))
    other = swap(packed, sibling, sibling)
    other_features = swap(features, sibling, sibling)

    local, states = pl.pallas_call(
        local_kernel,
        in_specs=[vmem()] * 5,
        out_specs=[vmem()] * 2,
        out_shape=[
            jax.ShapeDtypeStruct((2, 3, tokens, width), F32),
            jax.ShapeDtypeStruct((2, 2, HEADS, HS, HS), BF16),
        ],
    )(q, k, v, g, other)
    grads = pl.pallas_call(
        functools.partial(grads_kernel, scale=scale),
        in_specs=[smem()] + [vmem()] * 8,
        out_specs=vmem(),
        out_shape=jax.ShapeDtypeStruct((2, tokens, 3 * width), BF16),
    )(meta, k, v, g, other, local, states, near, far)

    part = functools.partial(weight_part, meta, features, other_features, grads, scale=weight_scale)
    here = swap(part(first=8, blocks=8), across, y)
    kept = part(first=0, blocks=8)
    for step, (core0, core1) in enumerate(((y, across), (z1, z1), (z2, z2))):
        half = kept.shape[0] // 2
        total = kept.astype(F32) + here.astype(F32)
        kept = total[:half]
        here = swap(total[half:].astype(BF16), core0, core1)
    final = (kept + here.astype(F32)).astype(BF16)[0]
    facing = swap(final, across, across)
    pair = swap(jnp.stack([final, facing]), sibling, sibling)
    weight_grad = pl.pallas_call(
        place_kernel,
        in_specs=[smem()] + [vmem()] * 3,
        out_specs=vmem(),
        out_shape=jax.ShapeDtypeStruct((seq_count * rows, 3 * width), F32),
    )(meta, final, facing, pair)
    return (grads[:1], weight_grad)


def solution(mesh):
    in_specs = (
        P("dp", "seq", None),
        P("dp", "seq", None),
        P("dp", "seq", None),
        P("dp", "seq", None),
        P("dp", "seq", None),
    )
    out_specs = (P("dp", "seq", None), P("dp", None))
    fast = mesh.shape["seq"] == 4 and mesh.shape["dp"] == 8
    body = on_device if fast else on_device_any
    return jax.shard_map(
        body, mesh=mesh, in_specs=in_specs, out_specs=out_specs, check_vma=False
    )
```

```python
import functools

import jax
import jax.numpy as jnp
from jax import lax
from jax.experimental import pallas as pl
from jax.experimental.pallas import tpu as pltpu
from jax.sharding import PartitionSpec as P

HS = 128
HEADS = 2
BLOCK = 128
BF16 = jnp.bfloat16
F32 = jnp.float32
AXES = ("seq", "dp")


def block_grads(query, key, value, grad_out, prefix, suffix, scale):
    count = query.shape[0]
    causal = jnp.arange(count)[:, None] >= jnp.arange(count)[None, :]
    f32 = jnp.float32
    score_a = jnp.einsum("thd,shd->hts", grad_out, value, preferred_element_type=f32)
    score_a = jnp.where(causal[None], score_a, 0.0).astype(jnp.bfloat16)
    score_b = jnp.einsum("thd,shd->hts", query, key, preferred_element_type=f32)
    score_b = jnp.where(causal[None], score_b, 0.0).astype(jnp.bfloat16)
    grad_q = jnp.einsum("hts,shd->thd", score_a, key, preferred_element_type=f32) + jnp.einsum(
        "thb,hab->tha", grad_out, prefix, preferred_element_type=f32
    )
    grad_k = jnp.einsum("htj,thd->jhd", score_a, query, preferred_element_type=f32) + jnp.einsum(
        "jhb,hab->jha", value, suffix, preferred_element_type=f32
    )
    grad_v = jnp.einsum("htj,thd->jhd", score_b, grad_out, preferred_element_type=f32) + jnp.einsum(
        "jha,hab->jhb", key, suffix, preferred_element_type=f32
    )
    joined = jnp.concatenate([grad_q, grad_k, grad_v], axis=1) * scale
    return joined.reshape(count, -1).astype(jnp.bfloat16)


def on_device_any(inputs, queries, keys, values, out_grad):
    tokens = queries.shape[1]
    seq_count = lax.axis_size("seq")
    batch_count = lax.axis_size("dp")
    length_all = tokens * seq_count
    scale = 1.0 / jnp.sqrt(jnp.float32(HS * length_all))
    weight_scale = 1.0 / jnp.sqrt(jnp.float32(batch_count * length_all))
    shape = (tokens, HEADS, HS)
    query = queries[0].reshape(shape)
    key = keys[0].reshape(shape)
    value = values[0].reshape(shape)
    grad_out = out_grad[0].reshape(shape)
    kv_state = jnp.einsum("lhi,lhj->hij", key, value, preferred_element_type=jnp.float32).astype(
        jnp.bfloat16
    )
    dq_state = jnp.einsum(
        "lhi,lhj->hij", query, grad_out, preferred_element_type=jnp.float32
    ).astype(jnp.bfloat16)
    stacked = jnp.stack([kv_state, dq_state])[None]
    position = lax.axis_index("seq")
    piece = lax.all_gather(stacked, "seq", axis=0, tiled=True)
    owners = jnp.arange(piece.shape[0])
    lower = (owners < position).astype(jnp.float32)
    higher = (owners > position).astype(jnp.float32)
    wide = piece.astype(jnp.float32)
    prefix = jnp.einsum("n,nhij->hij", lower, wide[:, 0])
    suffix = jnp.einsum("n,nhij->hij", higher, wide[:, 1])
    prefix = prefix.astype(jnp.bfloat16)
    suffix = suffix.astype(jnp.bfloat16)
    grads = block_grads(query, key, value, grad_out, prefix, suffix, scale)
    features = inputs[0]
    rows_here = lax.psum_scatter(
        (
            lax.dot_general(
                features, grads, (((0,), (0,)), ((), ())), preferred_element_type=jnp.float32
            )
            * weight_scale
        ).astype(jnp.bfloat16),
        "dp",
        scatter_dimension=0,
        tiled=True,
    )
    weight_grad = lax.psum(rows_here, "seq").astype(jnp.float32)
    return (grads[None], weight_grad)


def dot(a, b, a_dim=1, b_dim=0):
    return lax.dot_general(a, b, (((a_dim,), (b_dim,)), ((), ())), preferred_element_type=F32)


def cols(h):
    return slice(h * HS, (h + 1) * HS)


def vmem():
    return pl.BlockSpec(memory_space=pltpu.VMEM)


def smem():
    return pl.BlockSpec(memory_space=pltpu.SMEM)


def anywhere():
    return pl.BlockSpec(memory_space=pl.ANY)


def state_kernel(meta, q, k, v, g, send):
    upper = meta[1] == 1
    for h in range(HEADS):
        left = jnp.where(upper, q[:, cols(h)], k[:, cols(h)])
        right = jnp.where(upper, g[:, cols(h)], v[:, cols(h)])
        send[h] = dot(left, right, 0, 0).astype(BF16)


def local_kernel(q0, k0, v0, g0, q1, k1, v1, g1, local, turned, states):
    count = q0.shape[0]
    row = lax.broadcasted_iota(jnp.int32, (count, count), 0)
    col = lax.broadcasted_iota(jnp.int32, (count, count), 1)
    causal = row >= col
    causal_turned = row <= col
    for b, (q, k, v, g) in enumerate(((q0, k0, v0, g0), (q1, k1, v1, g1))):
        for h in range(HEADS):
            qh, kh, vh, gh = (ref[:, cols(h)] for ref in (q, k, v, g))
            qt, kt, vt, gt = qh.T, kh.T, vh.T, gh.T
            a_turned = jnp.where(causal_turned, dot(vh, gt), 0.0).astype(BF16)
            a = jnp.where(causal, dot(gh, vt), 0.0).astype(BF16)
            s = jnp.where(causal, dot(qh, kt), 0.0).astype(BF16)
            local[b, 0, cols(h)] = dot(kt, a_turned)
            local[b, 1, cols(h)] = dot(qt, a)
            local[b, 2, cols(h)] = dot(gt, s)
            states[b, 0, h] = dot(kt, vh).astype(BF16)
            states[b, 1, h] = dot(qt, gh).astype(BF16)
            turned[b, 0, h] = gt
            turned[b, 1, h] = vt
            turned[b, 2, h] = kt


def column_copies(table, first, x0, x1, held, sems):
    copies = []
    for b, x in enumerate((x0, x1)):
        for i in range(8):
            start = pl.multiple_of(table[4 + first + i] * BLOCK, BLOCK)
            copies.append(
                pltpu.make_async_copy(
                    x.at[:, pl.ds(start, BLOCK)],
                    held.at[b, :, pl.ds(i * BLOCK, BLOCK)],
                    sems.at[b, i],
                )
            )
    return copies


def weights(grads, held, out):
    for i in range(0, 8, 2):
        span = slice(i * BLOCK, (i + 2) * BLOCK)
        total = dot(grads[0], held[0, :, span]) + dot(grads[1], held[1, :, span])
        out[i] = total[:, :BLOCK].astype(BF16)
        out[i + 1] = total[:, BLOCK:].astype(BF16)


def send_kernel(meta, local, turned, states, near, far, x0, x1, grads, out, held, sems, *, scale):
    copies = column_copies(meta, 8, x0, x1, held, sems)
    for copy in copies:
        copy.start()
    core = meta[0].astype(F32)
    upper = meta[1].astype(F32)
    width = HEADS * HS
    for h in range(HEADS):
        outside = near[h].astype(F32) + far[h].astype(F32)
        before = outside * upper
        after = outside * (1.0 - upper)
        for b in range(2):
            late = core if b == 0 else 1.0 - core
            prefix = (before + states[1 - b, 0, h].astype(F32) * late).astype(BF16)
            suffix = (after + states[1 - b, 1, h].astype(F32) * (1.0 - late)).astype(BF16)
            extra = (
                dot(prefix, turned[b, 0, h]),
                dot(suffix, turned[b, 1, h]),
                dot(suffix, turned[b, 2, h], 0, 0),
            )
            for part in range(3):
                total = (local[b, part, cols(h)] + extra[part]) * scale
                grads[b, part * width + h * HS : part * width + (h + 1) * HS] = total.astype(BF16)
    for copy in copies:
        copy.wait()
    weights(grads, held, out)


def keep_kernel(meta, grads, x0, x1, out, own, held, sems):
    copies = column_copies(meta, 0, x0, x1, held, sems)
    for copy in copies:
        copy.start()
    for i in range(0, grads.shape[1], HS):
        own[:, i : i + HS] = grads[0, i : i + HS].T
    for copy in copies:
        copy.wait()
    weights(grads, held, out)


def place_kernel(meta, own, near, pair, out):
    mine = meta[2]
    for turn, block in ((0, own[...]), (2, near[...]), (1, pair[0]), (3, pair[1])):
        start = pl.multiple_of((mine ^ turn) * BLOCK, BLOCK)
        out[pl.ds(start, BLOCK), :] = block.astype(F32)


def final_kernel(kept, here, out, *, scale):
    total = (kept[0].astype(F32) + here[0].astype(F32)) * scale
    out[...] = total.T.astype(BF16)


def partners(core0, core1, seq_count, dp_count):
    pairs = []
    for s in range(seq_count):
        for d in range(dp_count):
            ds, dd = (core0, core1)[s % 2]
            pairs.append((s * dp_count + d, (s ^ ds) * dp_count + (d ^ dd)))
    return pairs


def on_device(inputs, queries, keys, values, out_grad):
    tokens = queries.shape[1]
    seq_count = lax.axis_size("seq")
    dp_count = lax.axis_size("dp")
    length_all = tokens * seq_count
    scale = float(1.0 / (HS * length_all) ** 0.5)
    weight_scale = float(1.0 / (dp_count * length_all) ** 0.5)
    features = inputs[0]
    blocks = [value[0] for value in (queries, keys, values, out_grad)]
    width = blocks[0].shape[1]
    rows = features.shape[1] // (seq_count * dp_count)

    swap = lambda value, core0, core1: lax.ppermute(
        value, AXES, partners(core0, core1, seq_count, dp_count)
    )
    sibling, across, y, z1, z2 = (1, 0), (2, 0), (0, 1), (0, 2), (0, 4)

    s, d = lax.axis_index("seq"), lax.axis_index("dp")
    core, upper = s & 1, s >> 1
    lane = jnp.arange(20, dtype=jnp.int32)
    bits = lane - 4
    b1, b2, b3, b4 = (bits >> 3) & 1, (bits >> 2) & 1, (bits >> 1) & 1, bits & 1
    row_s = s ^ (2 * jnp.where(core == 0, b1, b2))
    row_d = d ^ jnp.where(core == 0, b3, b1) ^ (2 * jnp.where(core == 0, b2, b3)) ^ (4 * b4)
    place = row_d * seq_count + row_s
    meta = jnp.where(
        lane == 0, core, jnp.where(lane == 1, upper, jnp.where(lane == 2, s, place))
    ).astype(jnp.int32)

    others = [swap(value, sibling, sibling) for value in blocks]
    send = pl.pallas_call(
        state_kernel,
        in_specs=[smem()] + [vmem()] * 4,
        out_specs=vmem(),
        out_shape=jax.ShapeDtypeStruct((HEADS, HS, HS), BF16),
    )(meta, *blocks)
    near = swap(send, across, across)
    far = swap(send, (3, 0), (3, 0))
    other_features = swap(features, sibling, sibling)

    local, turned, states = pl.pallas_call(
        local_kernel,
        in_specs=[vmem()] * 8,
        out_specs=[vmem()] * 3,
        out_shape=[
            jax.ShapeDtypeStruct((2, 3, width, tokens), F32),
            jax.ShapeDtypeStruct((2, 3, HEADS, HS, tokens), BF16),
            jax.ShapeDtypeStruct((2, 2, HEADS, HS, HS), BF16),
        ],
    )(*blocks, *others)
    half = jax.ShapeDtypeStruct((8, 3 * width, BLOCK), BF16)
    scratch = [pltpu.VMEM((2, tokens, 8 * BLOCK), BF16), pltpu.SemaphoreType.DMA((2, 8))]
    grads, going = pl.pallas_call(
        functools.partial(send_kernel, scale=scale),
        in_specs=[smem()] + [vmem()] * 5 + [anywhere()] * 2,
        out_specs=[vmem()] * 2,
        out_shape=[jax.ShapeDtypeStruct((2, 3 * width, tokens), BF16), half],
        scratch_shapes=scratch,
    )(meta, local, turned, states, near, far, features, other_features)
    here = swap(going, across, y)
    kept, own = pl.pallas_call(
        keep_kernel,
        in_specs=[smem(), vmem()] + [anywhere()] * 2,
        out_specs=[vmem()] * 2,
        out_shape=[half, jax.ShapeDtypeStruct((tokens, 3 * width), BF16)],
        scratch_shapes=scratch,
    )(meta, grads, features, other_features)
    for core0, core1 in ((z1, across), (y, z1), (z2, z2)):
        count = kept.shape[0] // 2
        total = kept.astype(F32) + here.astype(F32)
        kept = total[:count]
        here = swap(total[count:].astype(BF16), core0, core1)
    final = pl.pallas_call(
        functools.partial(final_kernel, scale=weight_scale),
        in_specs=[vmem()] * 2,
        out_specs=vmem(),
        out_shape=jax.ShapeDtypeStruct((BLOCK, 3 * width), BF16),
    )(kept, here)
    facing = swap(final, across, across)
    pair = swap(jnp.stack([final, facing]), sibling, sibling)
    weight_grad = pl.pallas_call(
        place_kernel,
        in_specs=[smem()] + [vmem()] * 3,
        out_specs=vmem(),
        out_shape=jax.ShapeDtypeStruct((seq_count * rows, 3 * width), F32),
    )(meta, final, facing, pair)
    return (own[None], weight_grad)


def solution(mesh):
    in_specs = (
        P("dp", "seq", None),
        P("dp", "seq", None),
        P("dp", "seq", None),
        P("dp", "seq", None),
        P("dp", "seq", None),
    )
    out_specs = (P("dp", "seq", None), P("dp", None))
    fast = mesh.shape["seq"] == 4 and mesh.shape["dp"] == 8
    body = on_device if fast else on_device_any
    return jax.shard_map(
        body, mesh=mesh, in_specs=in_specs, out_specs=out_specs, check_vma=False
    )
```

```python
import functools

import jax
import jax.numpy as jnp
from jax import lax
from jax.experimental import pallas as pl
from jax.experimental.pallas import tpu as pltpu
from jax.sharding import PartitionSpec as P

HS = 128
HEADS = 2
BLOCK = 128
BF16 = jnp.bfloat16
F32 = jnp.float32
AXES = ("seq", "dp")


def block_grads(query, key, value, grad_out, prefix, suffix, scale):
    count = query.shape[0]
    causal = jnp.arange(count)[:, None] >= jnp.arange(count)[None, :]
    f32 = jnp.float32
    score_a = jnp.einsum("thd,shd->hts", grad_out, value, preferred_element_type=f32)
    score_a = jnp.where(causal[None], score_a, 0.0).astype(jnp.bfloat16)
    score_b = jnp.einsum("thd,shd->hts", query, key, preferred_element_type=f32)
    score_b = jnp.where(causal[None], score_b, 0.0).astype(jnp.bfloat16)
    grad_q = jnp.einsum("hts,shd->thd", score_a, key, preferred_element_type=f32) + jnp.einsum(
        "thb,hab->tha", grad_out, prefix, preferred_element_type=f32
    )
    grad_k = jnp.einsum("htj,thd->jhd", score_a, query, preferred_element_type=f32) + jnp.einsum(
        "jhb,hab->jha", value, suffix, preferred_element_type=f32
    )
    grad_v = jnp.einsum("htj,thd->jhd", score_b, grad_out, preferred_element_type=f32) + jnp.einsum(
        "jha,hab->jhb", key, suffix, preferred_element_type=f32
    )
    joined = jnp.concatenate([grad_q, grad_k, grad_v], axis=1) * scale
    return joined.reshape(count, -1).astype(jnp.bfloat16)


def on_device_any(inputs, queries, keys, values, out_grad):
    tokens = queries.shape[1]
    seq_count = lax.axis_size("seq")
    batch_count = lax.axis_size("dp")
    length_all = tokens * seq_count
    scale = 1.0 / jnp.sqrt(jnp.float32(HS * length_all))
    weight_scale = 1.0 / jnp.sqrt(jnp.float32(batch_count * length_all))
    shape = (tokens, HEADS, HS)
    query = queries[0].reshape(shape)
    key = keys[0].reshape(shape)
    value = values[0].reshape(shape)
    grad_out = out_grad[0].reshape(shape)
    kv_state = jnp.einsum("lhi,lhj->hij", key, value, preferred_element_type=jnp.float32).astype(
        jnp.bfloat16
    )
    dq_state = jnp.einsum(
        "lhi,lhj->hij", query, grad_out, preferred_element_type=jnp.float32
    ).astype(jnp.bfloat16)
    stacked = jnp.stack([kv_state, dq_state])[None]
    position = lax.axis_index("seq")
    piece = lax.all_gather(stacked, "seq", axis=0, tiled=True)
    owners = jnp.arange(piece.shape[0])
    lower = (owners < position).astype(jnp.float32)
    higher = (owners > position).astype(jnp.float32)
    wide = piece.astype(jnp.float32)
    prefix = jnp.einsum("n,nhij->hij", lower, wide[:, 0])
    suffix = jnp.einsum("n,nhij->hij", higher, wide[:, 1])
    prefix = prefix.astype(jnp.bfloat16)
    suffix = suffix.astype(jnp.bfloat16)
    grads = block_grads(query, key, value, grad_out, prefix, suffix, scale)
    features = inputs[0]
    rows_here = lax.psum_scatter(
        (
            lax.dot_general(
                features, grads, (((0,), (0,)), ((), ())), preferred_element_type=jnp.float32
            )
            * weight_scale
        ).astype(jnp.bfloat16),
        "dp",
        scatter_dimension=0,
        tiled=True,
    )
    weight_grad = lax.psum(rows_here, "seq").astype(jnp.float32)
    return (grads[None], weight_grad)


def dot(a, b, a_dim=1, b_dim=0):
    return lax.dot_general(a, b, (((a_dim,), (b_dim,)), ((), ())), preferred_element_type=F32)


def cols(h):
    return slice(h * HS, (h + 1) * HS)


def vmem():
    return pl.BlockSpec(memory_space=pltpu.VMEM)


def smem():
    return pl.BlockSpec(memory_space=pltpu.SMEM)


def params(mebibytes):
    return pltpu.CompilerParams(vmem_limit_bytes=mebibytes << 20)


def hbm():
    return pl.BlockSpec(memory_space=pltpu.HBM)


def state_kernel(meta, q, k, v, g, send, held, sems):
    copies = [
        pltpu.make_async_copy(ref, held.at[i], sems.at[i]) for i, ref in enumerate((q, k, v, g))
    ]
    for copy in copies:
        copy.start()
    for copy in copies:
        copy.wait()
    upper = meta[1] == 1
    for h in range(HEADS):
        left = jnp.where(upper, held[0, :, cols(h)], held[1, :, cols(h)])
        right = jnp.where(upper, held[3, :, cols(h)], held[2, :, cols(h)])
        send[h] = dot(left, right, 0, 0).astype(BF16)


def local_kernel(mine, other, local, turned, states):
    count = mine.shape[1]
    row = lax.broadcasted_iota(jnp.int32, (count, count), 0)
    col = lax.broadcasted_iota(jnp.int32, (count, count), 1)
    causal = row >= col
    causal_turned = row <= col
    for b, (q, k, v, g) in enumerate(tuple(ref.at[i] for i in range(4)) for ref in (mine, other)):
        for h in range(HEADS):
            qh, kh, vh, gh = (ref[:, cols(h)] for ref in (q, k, v, g))
            qt, kt, vt, gt = qh.T, kh.T, vh.T, gh.T
            a_turned = jnp.where(causal_turned, dot(vh, gt), 0.0).astype(BF16)
            a = jnp.where(causal, dot(gh, vt), 0.0).astype(BF16)
            s = jnp.where(causal, dot(qh, kt), 0.0).astype(BF16)
            local[b, 0, cols(h)] = dot(kt, a_turned)
            local[b, 1, cols(h)] = dot(qt, a)
            local[b, 2, cols(h)] = dot(gt, s)
            states[b, 0, h] = dot(kt, vh).astype(BF16)
            states[b, 1, h] = dot(qt, gh).astype(BF16)
            turned[b, 0, h] = gt
            turned[b, 1, h] = vt
            turned[b, 2, h] = kt


def column(table, i):
    return pl.ds(pl.multiple_of(table[4 + i] * BLOCK, BLOCK), BLOCK)


def column_copies(table, first, x, held, sems):
    return [
        pltpu.make_async_copy(
            x.at[:, column(table, first + i)], held.at[:, pl.ds(i * BLOCK, BLOCK)], sems.at[i]
        )
        for i in range(8)
    ]


def weights(table, first, grads, held, x1, out):
    for i in range(0, 8, 2):
        span = slice(i * BLOCK, (i + 2) * BLOCK)
        other = jnp.concatenate([x1[:, column(table, first + i + j)] for j in range(2)], axis=1)
        total = dot(grads[0], held[:, span]) + dot(grads[1], other)
        out[i] = total[:, :BLOCK].astype(BF16)
        out[i + 1] = total[:, BLOCK:].astype(BF16)


def send_kernel(meta, local, turned, states, near, far, x0, x1, grads, out, held, sems, *, scale):
    copies = column_copies(meta, 8, x0, held, sems)
    for copy in copies:
        copy.start()
    core = meta[0].astype(F32)
    upper = meta[1].astype(F32)
    width = HEADS * HS
    for h in range(HEADS):
        outside = near[h].astype(F32) + far[h].astype(F32)
        before = outside * upper
        after = outside * (1.0 - upper)
        for b in range(2):
            late = core if b == 0 else 1.0 - core
            prefix = (before + states[1 - b, 0, h].astype(F32) * late).astype(BF16)
            suffix = (after + states[1 - b, 1, h].astype(F32) * (1.0 - late)).astype(BF16)
            extra = (
                dot(prefix, turned[b, 0, h]),
                dot(suffix, turned[b, 1, h]),
                dot(suffix, turned[b, 2, h], 0, 0),
            )
            for part in range(3):
                total = (local[b, part, cols(h)] + extra[part]) * scale
                grads[b, part * width + h * HS : part * width + (h + 1) * HS] = total.astype(BF16)
    for copy in copies:
        copy.wait()
    weights(meta, 8, grads, held, x1, out)


def keep_kernel(meta, grads, x0, x1, out, own, held, sems):
    copies = column_copies(meta, 0, x0, held, sems)
    for copy in copies:
        copy.start()
    for i in range(0, grads.shape[1], HS):
        own[:, i : i + HS] = grads[0, i : i + HS].T
    for copy in copies:
        copy.wait()
    weights(meta, 0, grads, held, x1, out)


def place_kernel(meta, own, near, pair, out):
    mine = meta[2]
    for turn, block in ((0, own[...]), (2, near[...]), (1, pair[0]), (3, pair[1])):
        start = pl.multiple_of((mine ^ turn) * BLOCK, BLOCK)
        out[pl.ds(start, BLOCK), :] = block.astype(F32)


def final_kernel(kept, here, out, *, scale):
    total = (kept[0].astype(F32) + here[0].astype(F32)) * scale
    out[...] = total.T.astype(BF16)


def partners(core0, core1, seq_count, dp_count):
    pairs = []
    for s in range(seq_count):
        for d in range(dp_count):
            ds, dd = (core0, core1)[s % 2]
            pairs.append((s * dp_count + d, (s ^ ds) * dp_count + (d ^ dd)))
    return pairs


def on_device(inputs, queries, keys, values, out_grad):
    tokens = queries.shape[1]
    seq_count = lax.axis_size("seq")
    dp_count = lax.axis_size("dp")
    length_all = tokens * seq_count
    scale = float(1.0 / (HS * length_all) ** 0.5)
    weight_scale = float(1.0 / (dp_count * length_all) ** 0.5)
    features = inputs[0]
    blocks = [value[0] for value in (queries, keys, values, out_grad)]
    stay = lambda value: pltpu.with_memory_space_constraint(value, pltpu.HBM)
    width = blocks[0].shape[1]
    rows = features.shape[1] // (seq_count * dp_count)

    swap = lambda value, core0, core1: lax.ppermute(
        value, AXES, partners(core0, core1, seq_count, dp_count)
    )
    sibling, across, y, z1, z2 = (1, 0), (2, 0), (0, 1), (0, 2), (0, 4)

    s, d = lax.axis_index("seq"), lax.axis_index("dp")
    core, upper = s & 1, s >> 1
    lane = jnp.arange(20, dtype=jnp.int32)
    bits = lane - 4
    b1, b2, b3, b4 = (bits >> 3) & 1, (bits >> 2) & 1, (bits >> 1) & 1, bits & 1
    row_s = s ^ (2 * jnp.where(core == 0, b1, b2))
    row_d = d ^ jnp.where(core == 0, b3, b1) ^ (2 * jnp.where(core == 0, b2, b3)) ^ (4 * b4)
    place = row_d * seq_count + row_s
    meta = jnp.where(
        lane == 0, core, jnp.where(lane == 1, upper, jnp.where(lane == 2, s, place))
    ).astype(jnp.int32)

    send, mine = pl.pallas_call(
        state_kernel,
        in_specs=[smem()] + [hbm()] * 4,
        out_specs=[vmem()] * 2,
        out_shape=[
            jax.ShapeDtypeStruct((HEADS, HS, HS), BF16),
            jax.ShapeDtypeStruct((4, tokens, width), BF16),
        ],
        scratch_shapes=[pltpu.SemaphoreType.DMA((4,))],
        compiler_params=params(4),
    )(meta, *map(stay, blocks))
    near = swap(send, across, across)
    far = swap(send, (3, 0), (3, 0))
    other = swap(mine, sibling, sibling)
    other_features = swap(features, sibling, sibling)

    local, turned, states = pl.pallas_call(
        local_kernel,
        in_specs=[vmem()] * 2,
        out_specs=[vmem()] * 3,
        out_shape=[
            jax.ShapeDtypeStruct((2, 3, width, tokens), F32),
            jax.ShapeDtypeStruct((2, 3, HEADS, HS, tokens), BF16),
            jax.ShapeDtypeStruct((2, 2, HEADS, HS, HS), BF16),
        ],
        compiler_params=params(16),
    )(mine, other)
    half = jax.ShapeDtypeStruct((8, 3 * width, BLOCK), BF16)
    scratch = [pltpu.VMEM((tokens, 8 * BLOCK), BF16), pltpu.SemaphoreType.DMA((8,))]
    grads, going = pl.pallas_call(
        functools.partial(send_kernel, scale=scale),
        in_specs=[smem()] + [vmem()] * 5 + [hbm(), vmem()],
        out_specs=[vmem()] * 2,
        out_shape=[jax.ShapeDtypeStruct((2, 3 * width, tokens), BF16), half],
        scratch_shapes=scratch,
        compiler_params=params(16),
    )(meta, local, turned, states, near, far, stay(features), other_features)
    here = swap(going, across, y)
    kept, own = pl.pallas_call(
        keep_kernel,
        in_specs=[smem(), vmem(), hbm(), vmem()],
        out_specs=[vmem()] * 2,
        out_shape=[half, jax.ShapeDtypeStruct((tokens, 3 * width), BF16)],
        scratch_shapes=scratch,
        compiler_params=params(16),
    )(meta, grads, stay(features), other_features)
    for core0, core1 in ((z1, across), (y, z1), (z2, z2)):
        count = kept.shape[0] // 2
        total = kept.astype(F32) + here.astype(F32)
        kept = total[:count]
        here = swap(total[count:].astype(BF16), core0, core1)
    final = pl.pallas_call(
        functools.partial(final_kernel, scale=weight_scale),
        in_specs=[vmem()] * 2,
        out_specs=vmem(),
        out_shape=jax.ShapeDtypeStruct((BLOCK, 3 * width), BF16),
        compiler_params=params(4),
    )(kept, here)
    facing = swap(final, across, across)
    pair = swap(jnp.stack([final, facing]), sibling, sibling)
    weight_grad = pl.pallas_call(
        place_kernel,
        in_specs=[smem()] + [vmem()] * 3,
        out_specs=vmem(),
        out_shape=jax.ShapeDtypeStruct((seq_count * rows, 3 * width), F32),
        compiler_params=params(8),
    )(meta, final, facing, pair)
    return (own[None], weight_grad)


def solution(mesh):
    in_specs = (
        P("dp", "seq", None),
        P("dp", "seq", None),
        P("dp", "seq", None),
        P("dp", "seq", None),
        P("dp", "seq", None),
    )
    out_specs = (P("dp", "seq", None), P("dp", None))
    fast = mesh.shape["seq"] == 4 and mesh.shape["dp"] == 8
    body = on_device if fast else on_device_any
    return jax.shard_map(
        body, mesh=mesh, in_specs=in_specs, out_specs=out_specs, check_vma=False
    )
```

```python
import functools

import jax
import jax.numpy as jnp
from jax import lax
from jax.experimental import pallas as pl
from jax.experimental.pallas import tpu as pltpu
from jax.sharding import PartitionSpec as P

HS = 128
HEADS = 2
BLOCK = 128
BF16 = jnp.bfloat16
F32 = jnp.float32
AXES = ("seq", "dp")


def block_grads(query, key, value, grad_out, prefix, suffix, scale):
    count = query.shape[0]
    causal = jnp.arange(count)[:, None] >= jnp.arange(count)[None, :]
    f32 = jnp.float32
    score_a = jnp.einsum("thd,shd->hts", grad_out, value, preferred_element_type=f32)
    score_a = jnp.where(causal[None], score_a, 0.0).astype(jnp.bfloat16)
    score_b = jnp.einsum("thd,shd->hts", query, key, preferred_element_type=f32)
    score_b = jnp.where(causal[None], score_b, 0.0).astype(jnp.bfloat16)
    grad_q = jnp.einsum("hts,shd->thd", score_a, key, preferred_element_type=f32) + jnp.einsum(
        "thb,hab->tha", grad_out, prefix, preferred_element_type=f32
    )
    grad_k = jnp.einsum("htj,thd->jhd", score_a, query, preferred_element_type=f32) + jnp.einsum(
        "jhb,hab->jha", value, suffix, preferred_element_type=f32
    )
    grad_v = jnp.einsum("htj,thd->jhd", score_b, grad_out, preferred_element_type=f32) + jnp.einsum(
        "jha,hab->jhb", key, suffix, preferred_element_type=f32
    )
    joined = jnp.concatenate([grad_q, grad_k, grad_v], axis=1) * scale
    return joined.reshape(count, -1).astype(jnp.bfloat16)


def on_device_any(inputs, queries, keys, values, out_grad):
    tokens = queries.shape[1]
    seq_count = lax.axis_size("seq")
    batch_count = lax.axis_size("dp")
    length_all = tokens * seq_count
    scale = 1.0 / jnp.sqrt(jnp.float32(HS * length_all))
    weight_scale = 1.0 / jnp.sqrt(jnp.float32(batch_count * length_all))
    shape = (tokens, HEADS, HS)
    query = queries[0].reshape(shape)
    key = keys[0].reshape(shape)
    value = values[0].reshape(shape)
    grad_out = out_grad[0].reshape(shape)
    kv_state = jnp.einsum("lhi,lhj->hij", key, value, preferred_element_type=jnp.float32).astype(
        jnp.bfloat16
    )
    dq_state = jnp.einsum(
        "lhi,lhj->hij", query, grad_out, preferred_element_type=jnp.float32
    ).astype(jnp.bfloat16)
    stacked = jnp.stack([kv_state, dq_state])[None]
    position = lax.axis_index("seq")
    piece = lax.all_gather(stacked, "seq", axis=0, tiled=True)
    owners = jnp.arange(piece.shape[0])
    lower = (owners < position).astype(jnp.float32)
    higher = (owners > position).astype(jnp.float32)
    wide = piece.astype(jnp.float32)
    prefix = jnp.einsum("n,nhij->hij", lower, wide[:, 0])
    suffix = jnp.einsum("n,nhij->hij", higher, wide[:, 1])
    prefix = prefix.astype(jnp.bfloat16)
    suffix = suffix.astype(jnp.bfloat16)
    grads = block_grads(query, key, value, grad_out, prefix, suffix, scale)
    features = inputs[0]
    rows_here = lax.psum_scatter(
        (
            lax.dot_general(
                features, grads, (((0,), (0,)), ((), ())), preferred_element_type=jnp.float32
            )
            * weight_scale
        ).astype(jnp.bfloat16),
        "dp",
        scatter_dimension=0,
        tiled=True,
    )
    weight_grad = lax.psum(rows_here, "seq").astype(jnp.float32)
    return (grads[None], weight_grad)


def dot(a, b, a_dim=1, b_dim=0):
    return lax.dot_general(a, b, (((a_dim,), (b_dim,)), ((), ())), preferred_element_type=F32)


def cols(h):
    return slice(h * HS, (h + 1) * HS)


def vmem():
    return pl.BlockSpec(memory_space=pltpu.VMEM)


def smem():
    return pl.BlockSpec(memory_space=pltpu.SMEM)


def params(mebibytes):
    return pltpu.CompilerParams(vmem_limit_bytes=mebibytes << 20)


def hbm():
    return pl.BlockSpec(memory_space=pltpu.HBM)


def state_kernel(meta, q, k, v, g, send, held, sems):
    copies = [
        pltpu.make_async_copy(ref, held.at[i], sems.at[i]) for i, ref in enumerate((q, k, v, g))
    ]
    for copy in copies:
        copy.start()
    for copy in copies:
        copy.wait()
    upper = meta[1] == 1
    for h in range(HEADS):
        left = jnp.where(upper, held[0, :, cols(h)], held[1, :, cols(h)])
        right = jnp.where(upper, held[3, :, cols(h)], held[2, :, cols(h)])
        send[h] = dot(left, right, 0, 0).astype(BF16)


def local_kernel(mine, other, local, turned, states):
    count = mine.shape[1]
    row = lax.broadcasted_iota(jnp.int32, (count, count), 0)
    col = lax.broadcasted_iota(jnp.int32, (count, count), 1)
    causal = row >= col
    causal_turned = row <= col
    for b, (q, k, v, g) in enumerate(tuple(ref.at[i] for i in range(4)) for ref in (mine, other)):
        for h in range(HEADS):
            qh, kh, vh, gh = (ref[:, cols(h)] for ref in (q, k, v, g))
            qt, kt, vt, gt = qh.T, kh.T, vh.T, gh.T
            a_turned = jnp.where(causal_turned, dot(vh, gt), 0.0).astype(BF16)
            a = jnp.where(causal, dot(gh, vt), 0.0).astype(BF16)
            s = jnp.where(causal, dot(qh, kt), 0.0).astype(BF16)
            local[b, 0, cols(h)] = dot(kt, a_turned)
            local[b, 1, cols(h)] = dot(qt, a)
            local[b, 2, cols(h)] = dot(gt, s)
            states[b, 0, h] = dot(kt, vh).astype(BF16)
            states[b, 1, h] = dot(qt, gh).astype(BF16)
            turned[b, 0, h] = gt
            turned[b, 1, h] = vt
            turned[b, 2, h] = kt


def column(table, i):
    return pl.ds(pl.multiple_of(table[4 + i] * BLOCK, BLOCK), BLOCK)


def column_copies(table, first, x, held, sems):
    return [
        pltpu.make_async_copy(
            x.at[:, column(table, 16 * part + first + i)],
            held.at[part, :, pl.ds(i * BLOCK, BLOCK)],
            sems.at[part, i],
        )
        for part in range(2)
        for i in range(8)
    ]


def weights(table, first, grads, held, x1, outs):
    row = 0
    for part, out in enumerate(outs):
        rows = slice(row, row + out.shape[1])
        row += out.shape[1]
        left, right = grads[0, rows], grads[1, rows]
        for i in range(0, 8, 2):
            own = held[part, :, i * BLOCK : (i + 2) * BLOCK]
            other = jnp.concatenate(
                [x1[:, column(table, 16 * part + first + i + j)] for j in range(2)], axis=1
            )
            total = dot(left, own) + dot(right, other)
            out[i] = total[:, :BLOCK].astype(BF16)
            out[i + 1] = total[:, BLOCK:].astype(BF16)


def send_kernel(meta, local, turned, states, near, far, x0, x1, grads, out_a, out_b, held, sems, *, scale):
    copies = column_copies(meta, 8, x0, held, sems)
    for copy in copies:
        copy.start()
    core = meta[0].astype(F32)
    upper = meta[1].astype(F32)
    width = HEADS * HS
    for h in range(HEADS):
        outside = near[h].astype(F32) + far[h].astype(F32)
        before = outside * upper
        after = outside * (1.0 - upper)
        for b in range(2):
            late = core if b == 0 else 1.0 - core
            prefix = (before + states[1 - b, 0, h].astype(F32) * late).astype(BF16)
            suffix = (after + states[1 - b, 1, h].astype(F32) * (1.0 - late)).astype(BF16)
            extra = (
                dot(prefix, turned[b, 0, h]),
                dot(suffix, turned[b, 1, h]),
                dot(suffix, turned[b, 2, h], 0, 0),
            )
            for part in range(3):
                total = (local[b, part, cols(h)] + extra[part]) * scale
                grads[b, part * width + h * HS : part * width + (h + 1) * HS] = total.astype(BF16)
    for copy in copies:
        copy.wait()
    weights(meta, 8, grads, held, x1, (out_a, out_b))


def keep_kernel(meta, grads, x0, x1, out_a, out_b, own, held, sems):
    copies = column_copies(meta, 0, x0, held, sems)
    for copy in copies:
        copy.start()
    for i in range(0, grads.shape[1], HS):
        own[:, i : i + HS] = grads[0, i : i + HS].T
    for copy in copies:
        copy.wait()
    weights(meta, 0, grads, held, x1, (out_a, out_b))


def place_kernel(meta, own, near, pair, out):
    mine = meta[2]
    for turn, block in ((0, own[...]), (2, near[...]), (1, pair[0]), (3, pair[1])):
        start = pl.multiple_of((mine ^ turn) * BLOCK, BLOCK)
        out[pl.ds(start, BLOCK), :] = block.astype(F32)


def final_kernel(kept_a, kept_b, here, out, *, scale):
    kept = jnp.concatenate([kept_a[0], kept_b[0]], axis=0)
    out[...] = ((kept + here[...].astype(F32)) * scale).T.astype(BF16)


def partners(core0, core1, seq_count, dp_count):
    pairs = []
    for s in range(seq_count):
        for d in range(dp_count):
            ds, dd = (core0, core1)[s % 2]
            pairs.append((s * dp_count + d, (s ^ ds) * dp_count + (d ^ dd)))
    return pairs


def on_device(inputs, queries, keys, values, out_grad):
    tokens = queries.shape[1]
    seq_count = lax.axis_size("seq")
    dp_count = lax.axis_size("dp")
    length_all = tokens * seq_count
    scale = float(1.0 / (HS * length_all) ** 0.5)
    weight_scale = float(1.0 / (dp_count * length_all) ** 0.5)
    features = inputs[0]
    blocks = [value[0] for value in (queries, keys, values, out_grad)]
    stay = lambda value: pltpu.with_memory_space_constraint(value, pltpu.HBM)
    width = blocks[0].shape[1]
    rows = features.shape[1] // (seq_count * dp_count)

    swap = lambda value, core0, core1: lax.ppermute(
        value, AXES, partners(core0, core1, seq_count, dp_count)
    )
    sibling, across, y, z1, z2 = (1, 0), (2, 0), (0, 1), (0, 2), (0, 4)

    s, d = lax.axis_index("seq"), lax.axis_index("dp")
    core, upper = s & 1, s >> 1
    lane = jnp.arange(36, dtype=jnp.int32)
    bits = (lane - 4) & 15
    b1, b2, b3, b4 = (bits >> 3) & 1, (bits >> 2) & 1, (bits >> 1) & 1, bits & 1
    lower, first = core == 0, lane < 20
    over_x = jnp.where(first, jnp.where(lower, b1, b2), b3)
    over_y = jnp.where(first, jnp.where(lower, b3, b1), b2)
    over_z = jnp.where(first, jnp.where(lower, b2, b3), b1)
    place = (d ^ over_y ^ (2 * over_z) ^ (4 * b4)) * seq_count + (s ^ (2 * over_x))
    meta = jnp.where(
        lane == 0, core, jnp.where(lane == 1, upper, jnp.where(lane == 2, s, place))
    ).astype(jnp.int32)

    send, mine = pl.pallas_call(
        state_kernel,
        in_specs=[smem()] + [hbm()] * 4,
        out_specs=[vmem()] * 2,
        out_shape=[
            jax.ShapeDtypeStruct((HEADS, HS, HS), BF16),
            jax.ShapeDtypeStruct((4, tokens, width), BF16),
        ],
        scratch_shapes=[pltpu.SemaphoreType.DMA((4,))],
        compiler_params=params(4),
    )(meta, *map(stay, blocks))
    near = swap(send, across, across)
    far = swap(send, (3, 0), (3, 0))
    other = swap(mine, sibling, sibling)
    other_features = swap(features, sibling, sibling)

    local, turned, states = pl.pallas_call(
        local_kernel,
        in_specs=[vmem()] * 2,
        out_specs=[vmem()] * 3,
        out_shape=[
            jax.ShapeDtypeStruct((2, 3, width, tokens), F32),
            jax.ShapeDtypeStruct((2, 3, HEADS, HS, tokens), BF16),
            jax.ShapeDtypeStruct((2, 2, HEADS, HS, HS), BF16),
        ],
        compiler_params=params(16),
    )(mine, other)
    halves = [
        jax.ShapeDtypeStruct((8, count * width, BLOCK), BF16) for count in (2, 1)
    ]
    scratch = [pltpu.VMEM((2, tokens, 8 * BLOCK), BF16), pltpu.SemaphoreType.DMA((2, 8))]
    grads, *going = pl.pallas_call(
        functools.partial(send_kernel, scale=scale),
        in_specs=[smem()] + [vmem()] * 5 + [hbm(), vmem()],
        out_specs=[vmem()] * 3,
        out_shape=[jax.ShapeDtypeStruct((2, 3 * width, tokens), BF16)] + halves,
        scratch_shapes=scratch,
        compiler_params=params(16),
    )(meta, local, turned, states, near, far, stay(features), other_features)
    here = [swap(going[0], across, y), swap(going[1], z1, z1)]
    *kept, own = pl.pallas_call(
        keep_kernel,
        in_specs=[smem(), vmem(), hbm(), vmem()],
        out_specs=[vmem()] * 3,
        out_shape=halves + [jax.ShapeDtypeStruct((tokens, 3 * width), BF16)],
        scratch_shapes=scratch,
        compiler_params=params(16),
    )(meta, grads, stay(features), other_features)
    for ways in (((z1, across), (y, y)), ((y, z1), (across, across))):
        for i, way in enumerate(ways):
            count = kept[i].shape[0] // 2
            total = kept[i].astype(F32) + here[i].astype(F32)
            kept[i] = total[:count]
            here[i] = swap(total[count:].astype(BF16), *way)
    total = [k + h.astype(F32) for k, h in zip(kept, here)]
    last = swap(jnp.concatenate([t[1] for t in total]).astype(BF16), z2, z2)
    final = pl.pallas_call(
        functools.partial(final_kernel, scale=weight_scale),
        in_specs=[vmem()] * 3,
        out_specs=vmem(),
        out_shape=jax.ShapeDtypeStruct((BLOCK, 3 * width), BF16),
        compiler_params=params(4),
    )(total[0][:1], total[1][:1], last)
    facing = swap(final, across, across)
    pair = swap(jnp.stack([final, facing]), sibling, sibling)
    weight_grad = pl.pallas_call(
        place_kernel,
        in_specs=[smem()] + [vmem()] * 3,
        out_specs=vmem(),
        out_shape=jax.ShapeDtypeStruct((seq_count * rows, 3 * width), F32),
        compiler_params=params(8),
    )(meta, final, facing, pair)
    return (own[None], weight_grad)


def solution(mesh):
    in_specs = (
        P("dp", "seq", None),
        P("dp", "seq", None),
        P("dp", "seq", None),
        P("dp", "seq", None),
        P("dp", "seq", None),
    )
    out_specs = (P("dp", "seq", None), P("dp", None))
    fast = mesh.shape["seq"] == 4 and mesh.shape["dp"] == 8
    body = on_device if fast else on_device_any
    return jax.shard_map(
        body, mesh=mesh, in_specs=in_specs, out_specs=out_specs, check_vma=False
    )
```

```python
import functools

import jax
import jax.numpy as jnp
from jax import lax
from jax.experimental import pallas as pl
from jax.experimental.pallas import tpu as pltpu
from jax.sharding import PartitionSpec as P

HS = 128
HEADS = 2
BLOCK = 128
BF16 = jnp.bfloat16
F32 = jnp.float32
AXES = ("seq", "dp")


def block_grads(query, key, value, grad_out, prefix, suffix, scale):
    count = query.shape[0]
    causal = jnp.arange(count)[:, None] >= jnp.arange(count)[None, :]
    f32 = jnp.float32
    score_a = jnp.einsum("thd,shd->hts", grad_out, value, preferred_element_type=f32)
    score_a = jnp.where(causal[None], score_a, 0.0).astype(jnp.bfloat16)
    score_b = jnp.einsum("thd,shd->hts", query, key, preferred_element_type=f32)
    score_b = jnp.where(causal[None], score_b, 0.0).astype(jnp.bfloat16)
    grad_q = jnp.einsum("hts,shd->thd", score_a, key, preferred_element_type=f32) + jnp.einsum(
        "thb,hab->tha", grad_out, prefix, preferred_element_type=f32
    )
    grad_k = jnp.einsum("htj,thd->jhd", score_a, query, preferred_element_type=f32) + jnp.einsum(
        "jhb,hab->jha", value, suffix, preferred_element_type=f32
    )
    grad_v = jnp.einsum("htj,thd->jhd", score_b, grad_out, preferred_element_type=f32) + jnp.einsum(
        "jha,hab->jhb", key, suffix, preferred_element_type=f32
    )
    joined = jnp.concatenate([grad_q, grad_k, grad_v], axis=1) * scale
    return joined.reshape(count, -1).astype(jnp.bfloat16)


def on_device_any(inputs, queries, keys, values, out_grad):
    tokens = queries.shape[1]
    seq_count = lax.axis_size("seq")
    batch_count = lax.axis_size("dp")
    length_all = tokens * seq_count
    scale = 1.0 / jnp.sqrt(jnp.float32(HS * length_all))
    weight_scale = 1.0 / jnp.sqrt(jnp.float32(batch_count * length_all))
    shape = (tokens, HEADS, HS)
    query = queries[0].reshape(shape)
    key = keys[0].reshape(shape)
    value = values[0].reshape(shape)
    grad_out = out_grad[0].reshape(shape)
    kv_state = jnp.einsum("lhi,lhj->hij", key, value, preferred_element_type=jnp.float32).astype(
        jnp.bfloat16
    )
    dq_state = jnp.einsum(
        "lhi,lhj->hij", query, grad_out, preferred_element_type=jnp.float32
    ).astype(jnp.bfloat16)
    stacked = jnp.stack([kv_state, dq_state])[None]
    position = lax.axis_index("seq")
    piece = lax.all_gather(stacked, "seq", axis=0, tiled=True)
    owners = jnp.arange(piece.shape[0])
    lower = (owners < position).astype(jnp.float32)
    higher = (owners > position).astype(jnp.float32)
    wide = piece.astype(jnp.float32)
    prefix = jnp.einsum("n,nhij->hij", lower, wide[:, 0])
    suffix = jnp.einsum("n,nhij->hij", higher, wide[:, 1])
    prefix = prefix.astype(jnp.bfloat16)
    suffix = suffix.astype(jnp.bfloat16)
    grads = block_grads(query, key, value, grad_out, prefix, suffix, scale)
    features = inputs[0]
    rows_here = lax.psum_scatter(
        (
            lax.dot_general(
                features, grads, (((0,), (0,)), ((), ())), preferred_element_type=jnp.float32
            )
            * weight_scale
        ).astype(jnp.bfloat16),
        "dp",
        scatter_dimension=0,
        tiled=True,
    )
    weight_grad = lax.psum(rows_here, "seq").astype(jnp.float32)
    return (grads[None], weight_grad)


def dot(a, b, a_dim=1, b_dim=0):
    return lax.dot_general(a, b, (((a_dim,), (b_dim,)), ((), ())), preferred_element_type=F32)


def cols(h):
    return slice(h * HS, (h + 1) * HS)


def vmem():
    return pl.BlockSpec(memory_space=pltpu.VMEM)


def smem():
    return pl.BlockSpec(memory_space=pltpu.SMEM)


def params(mebibytes):
    return pltpu.CompilerParams(vmem_limit_bytes=mebibytes << 20)


def hbm():
    return pl.BlockSpec(memory_space=pltpu.HBM)


def state_kernel(meta, q, k, v, g, send, held, sems):
    copies = [
        pltpu.make_async_copy(ref, held.at[i], sems.at[i]) for i, ref in enumerate((q, k, v, g))
    ]
    for copy in copies:
        copy.start()
    for copy in copies:
        copy.wait()
    upper = meta[1] == 1
    for h in range(HEADS):
        left = jnp.where(upper, held[0, :, cols(h)], held[1, :, cols(h)])
        right = jnp.where(upper, held[3, :, cols(h)], held[2, :, cols(h)])
        send[h] = dot(left, right, 0, 0).astype(BF16)


def local_kernel(x, mine, other, local, turned, states, x0, sem):
    copy = pltpu.make_async_copy(x, x0, sem)
    copy.start()
    count = mine.shape[1]
    row = lax.broadcasted_iota(jnp.int32, (count, count), 0)
    col = lax.broadcasted_iota(jnp.int32, (count, count), 1)
    causal = row >= col
    causal_turned = row <= col
    for b, (q, k, v, g) in enumerate(tuple(ref.at[i] for i in range(4)) for ref in (mine, other)):
        for h in range(HEADS):
            qh, kh, vh, gh = (ref[:, cols(h)] for ref in (q, k, v, g))
            qt, kt, vt, gt = qh.T, kh.T, vh.T, gh.T
            a_turned = jnp.where(causal_turned, dot(vh, gt), 0.0).astype(BF16)
            a = jnp.where(causal, dot(gh, vt), 0.0).astype(BF16)
            s = jnp.where(causal, dot(qh, kt), 0.0).astype(BF16)
            local[b, 0, cols(h)] = dot(kt, a_turned)
            local[b, 1, cols(h)] = dot(qt, a)
            local[b, 2, cols(h)] = dot(gt, s)
            states[b, 0, h] = dot(kt, vh).astype(BF16)
            states[b, 1, h] = dot(qt, gh).astype(BF16)
            turned[b, 0, h] = gt
            turned[b, 1, h] = vt
            turned[b, 2, h] = kt
    copy.wait()


def column(table, i):
    return pl.ds(pl.multiple_of(table[4 + i] * BLOCK, BLOCK), BLOCK)


def weights(table, first, grads, x0, x1, out):
    for i in range(0, 8, 2):
        x = jnp.concatenate(
            [
                jnp.concatenate([ref[:, column(table, first + i + j)] for j in range(2)], axis=1)
                for ref in (x0, x1)
            ],
            axis=0,
        )
        total = dot(grads, x)
        out[i] = total[:, :BLOCK].astype(BF16)
        out[i + 1] = total[:, BLOCK:].astype(BF16)


def send_a_kernel(meta, local, turned, states, near, far, x0, x1, grads, out, *, scale):
    core = meta[0].astype(F32)
    upper = meta[1].astype(F32)
    width = HEADS * HS
    tokens = x0.shape[0]
    for h in range(HEADS):
        outside = near[h].astype(F32) + far[h].astype(F32)
        before = outside * upper
        after = outside * (1.0 - upper)
        for b in range(2):
            late = core if b == 0 else 1.0 - core
            prefix = (before + states[1 - b, 0, h].astype(F32) * late).astype(BF16)
            suffix = (after + states[1 - b, 1, h].astype(F32) * (1.0 - late)).astype(BF16)
            extra = (
                dot(prefix, turned[b, 0, h]),
                dot(suffix, turned[b, 1, h]),
                dot(suffix, turned[b, 2, h], 0, 0),
            )
            for part in range(3):
                total = (local[b, part, cols(h)] + extra[part]) * scale
                rows = slice(part * width + h * HS, part * width + (h + 1) * HS)
                grads[rows, b * tokens : (b + 1) * tokens] = total.astype(BF16)
    weights(meta, 8, grads[: 2 * width], x0, x1, out)


def send_b_kernel(meta, grads, x0, x1, out):
    weights(meta, 24, grads[2 * HEADS * HS :], x0, x1, out)


def keep_kernel(meta, grads, x0, x1, out_a, out_b, own):
    width = HEADS * HS
    weights(meta, 0, grads[: 2 * width], x0, x1, out_a)
    weights(meta, 16, grads[2 * width :], x0, x1, out_b)
    for i in range(0, grads.shape[0], HS):
        own[:, i : i + HS] = grads[i : i + HS, : own.shape[0]].T


def place_kernel(meta, *refs):
    out = refs[-1]
    column = 0
    for part in range(0, 8, 4):
        for turn, block in zip((0, 2, 1, 3), refs[part : part + 4]):
            rows = pl.ds(pl.multiple_of((meta[2] ^ turn) * BLOCK, BLOCK), BLOCK)
            out[rows, column : column + block.shape[1]] = block[...].astype(F32)
        column += refs[part].shape[1]


def final_kernel(total, here, out, *, scale):
    out[...] = ((total[0] + here[0].astype(F32)) * scale).T.astype(BF16)


def after(value, *others):
    return lax.optimization_barrier((value, *others))[0]


def partners(core0, core1, seq_count, dp_count):
    pairs = []
    for s in range(seq_count):
        for d in range(dp_count):
            ds, dd = (core0, core1)[s % 2]
            pairs.append((s * dp_count + d, (s ^ ds) * dp_count + (d ^ dd)))
    return pairs


def on_device(inputs, queries, keys, values, out_grad):
    tokens = queries.shape[1]
    seq_count = lax.axis_size("seq")
    dp_count = lax.axis_size("dp")
    length_all = tokens * seq_count
    scale = float(1.0 / (HS * length_all) ** 0.5)
    weight_scale = float(1.0 / (dp_count * length_all) ** 0.5)
    features = inputs[0]
    blocks = [value[0] for value in (queries, keys, values, out_grad)]
    stay = lambda value: pltpu.with_memory_space_constraint(value, pltpu.HBM)
    width = blocks[0].shape[1]
    rows = features.shape[1] // (seq_count * dp_count)

    swap = lambda value, core0, core1: lax.ppermute(
        value, AXES, partners(core0, core1, seq_count, dp_count)
    )
    sibling, across, y, z1, z2 = (1, 0), (2, 0), (0, 1), (0, 2), (0, 4)

    s, d = lax.axis_index("seq"), lax.axis_index("dp")
    core, upper = s & 1, s >> 1
    lane = jnp.arange(36, dtype=jnp.int32)
    bits = (lane - 4) & 15
    b1, b2, b3, b4 = (bits >> 3) & 1, (bits >> 2) & 1, (bits >> 1) & 1, bits & 1
    lower, first = core == 0, lane < 20
    over_x = jnp.where(first, jnp.where(lower, b1, b2), b3)
    over_y = jnp.where(first, jnp.where(lower, b3, b1), b2)
    over_z = jnp.where(first, jnp.where(lower, b2, b3), b1)
    spot = (d ^ over_y ^ (2 * over_z) ^ (4 * b4)) * seq_count + (s ^ (2 * over_x))
    meta = jnp.where(
        lane == 0, core, jnp.where(lane == 1, upper, jnp.where(lane == 2, s, spot))
    ).astype(jnp.int32)

    send, mine = pl.pallas_call(
        state_kernel,
        in_specs=[smem()] + [hbm()] * 4,
        out_specs=[vmem()] * 2,
        out_shape=[
            jax.ShapeDtypeStruct((HEADS, HS, HS), BF16),
            jax.ShapeDtypeStruct((4, tokens, width), BF16),
        ],
        scratch_shapes=[pltpu.SemaphoreType.DMA((4,))],
        compiler_params=params(4),
    )(meta, *map(stay, blocks))
    near = swap(send, across, across)
    other = swap(mine, sibling, sibling)
    other_x = swap(features, sibling, sibling)

    local, turned, states, mine_x = pl.pallas_call(
        local_kernel,
        in_specs=[hbm()] + [vmem()] * 2,
        out_specs=[vmem()] * 4,
        out_shape=[
            jax.ShapeDtypeStruct((2, 3, width, tokens), F32),
            jax.ShapeDtypeStruct((2, 3, HEADS, HS, tokens), BF16),
            jax.ShapeDtypeStruct((2, 2, HEADS, HS, HS), BF16),
            jax.ShapeDtypeStruct(features.shape, BF16),
        ],
        scratch_shapes=[pltpu.SemaphoreType.DMA],
        compiler_params=params(16),
    )(stay(features), mine, other)
    near = after(near, states)
    far = swap(near, sibling, sibling)
    halves = [
        jax.ShapeDtypeStruct((8, count * width, BLOCK), BF16) for count in (2, 1)
    ]
    grads, going_a = pl.pallas_call(
        functools.partial(send_a_kernel, scale=scale),
        in_specs=[smem()] + [vmem()] * 7,
        out_specs=[vmem()] * 2,
        out_shape=[jax.ShapeDtypeStruct((3 * width, 2 * tokens), BF16), halves[0]],
        compiler_params=params(16),
    )(meta, local, turned, states, near, far, mine_x, other_x)
    here_a = swap(going_a, across, y)
    going_b = pl.pallas_call(
        send_b_kernel,
        in_specs=[smem()] + [vmem()] * 3,
        out_specs=vmem(),
        out_shape=halves[1],
        compiler_params=params(16),
    )(meta, grads, mine_x, other_x)
    here = [here_a, swap(going_b, z1, z1)]
    *kept, own = pl.pallas_call(
        keep_kernel,
        in_specs=[smem()] + [vmem()] * 3,
        out_specs=[vmem()] * 3,
        out_shape=halves + [jax.ShapeDtypeStruct((tokens, 3 * width), BF16)],
        compiler_params=params(16),
    )(meta, grads, mine_x, other_x)

    def step(kept, here, way):
        count = kept.shape[0] // 2
        total = kept.astype(F32) + here.astype(F32)
        going = total[count:].astype(BF16)
        return total[:count], going, swap(going, *way)

    def finish(kept, here):
        final = pl.pallas_call(
            functools.partial(final_kernel, scale=weight_scale),
            in_specs=[vmem()] * 2,
            out_specs=vmem(),
            out_shape=jax.ShapeDtypeStruct((BLOCK, kept.shape[1]), BF16),
            compiler_params=params(4),
        )(kept, here)
        facing = swap(final, across, across)
        return final, facing, swap(final, sibling, sibling), swap(facing, sibling, sibling)

    kept_a, kept_b = kept
    here_a, here_b = here
    kept_a, going_a, here_a = step(kept_a, after(here_a, going_b, kept_a), (z1, across))
    kept_b, going_b, here_b = step(kept_b, after(here_b, going_a), (y, y))
    kept_b, going_b, here_b = step(kept_b, here_b, (across, across))
    kept_a, going_a, here_a = step(kept_a, after(here_a, going_b), (y, z1))
    kept_b, going_b, here_b = step(kept_b, after(here_b, going_a), (z2, z2))
    kept_a, going_a, here_a = step(kept_a, after(here_a, going_b), (z2, z2))
    part_b = finish(kept_b, after(here_b, going_a))
    part_a = finish(kept_a, after(here_a, part_b[1]))
    weight_grad = pl.pallas_call(
        place_kernel,
        in_specs=[smem()] + [vmem()] * 8,
        out_specs=vmem(),
        out_shape=jax.ShapeDtypeStruct((seq_count * rows, 3 * width), F32),
        compiler_params=params(8),
    )(meta, *part_a, *part_b)
    return (own[None], weight_grad)


def solution(mesh):
    in_specs = (
        P("dp", "seq", None),
        P("dp", "seq", None),
        P("dp", "seq", None),
        P("dp", "seq", None),
        P("dp", "seq", None),
    )
    out_specs = (P("dp", "seq", None), P("dp", None))
    fast = mesh.shape["seq"] == 4 and mesh.shape["dp"] == 8
    body = on_device if fast else on_device_any
    return jax.shard_map(
        body, mesh=mesh, in_specs=in_specs, out_specs=out_specs, check_vma=False
    )
```

```python
import functools

import jax
import jax.numpy as jnp
from jax import lax
from jax.experimental import pallas as pl
from jax.experimental.pallas import tpu as pltpu
from jax.sharding import PartitionSpec as P

HS = 128
HEADS = 2
BLOCK = 128
BF16 = jnp.bfloat16
F32 = jnp.float32
AXES = ("seq", "dp")


def block_grads(query, key, value, grad_out, prefix, suffix, scale):
    count = query.shape[0]
    causal = jnp.arange(count)[:, None] >= jnp.arange(count)[None, :]
    f32 = jnp.float32
    score_a = jnp.einsum("thd,shd->hts", grad_out, value, preferred_element_type=f32)
    score_a = jnp.where(causal[None], score_a, 0.0).astype(jnp.bfloat16)
    score_b = jnp.einsum("thd,shd->hts", query, key, preferred_element_type=f32)
    score_b = jnp.where(causal[None], score_b, 0.0).astype(jnp.bfloat16)
    grad_q = jnp.einsum("hts,shd->thd", score_a, key, preferred_element_type=f32) + jnp.einsum(
        "thb,hab->tha", grad_out, prefix, preferred_element_type=f32
    )
    grad_k = jnp.einsum("htj,thd->jhd", score_a, query, preferred_element_type=f32) + jnp.einsum(
        "jhb,hab->jha", value, suffix, preferred_element_type=f32
    )
    grad_v = jnp.einsum("htj,thd->jhd", score_b, grad_out, preferred_element_type=f32) + jnp.einsum(
        "jha,hab->jhb", key, suffix, preferred_element_type=f32
    )
    joined = jnp.concatenate([grad_q, grad_k, grad_v], axis=1) * scale
    return joined.reshape(count, -1).astype(jnp.bfloat16)


def on_device_any(inputs, queries, keys, values, out_grad):
    tokens = queries.shape[1]
    seq_count = lax.axis_size("seq")
    batch_count = lax.axis_size("dp")
    length_all = tokens * seq_count
    scale = 1.0 / jnp.sqrt(jnp.float32(HS * length_all))
    weight_scale = 1.0 / jnp.sqrt(jnp.float32(batch_count * length_all))
    shape = (tokens, HEADS, HS)
    query = queries[0].reshape(shape)
    key = keys[0].reshape(shape)
    value = values[0].reshape(shape)
    grad_out = out_grad[0].reshape(shape)
    kv_state = jnp.einsum("lhi,lhj->hij", key, value, preferred_element_type=jnp.float32).astype(
        jnp.bfloat16
    )
    dq_state = jnp.einsum(
        "lhi,lhj->hij", query, grad_out, preferred_element_type=jnp.float32
    ).astype(jnp.bfloat16)
    stacked = jnp.stack([kv_state, dq_state])[None]
    position = lax.axis_index("seq")
    piece = lax.all_gather(stacked, "seq", axis=0, tiled=True)
    owners = jnp.arange(piece.shape[0])
    lower = (owners < position).astype(jnp.float32)
    higher = (owners > position).astype(jnp.float32)
    wide = piece.astype(jnp.float32)
    prefix = jnp.einsum("n,nhij->hij", lower, wide[:, 0])
    suffix = jnp.einsum("n,nhij->hij", higher, wide[:, 1])
    prefix = prefix.astype(jnp.bfloat16)
    suffix = suffix.astype(jnp.bfloat16)
    grads = block_grads(query, key, value, grad_out, prefix, suffix, scale)
    features = inputs[0]
    rows_here = lax.psum_scatter(
        (
            lax.dot_general(
                features, grads, (((0,), (0,)), ((), ())), preferred_element_type=jnp.float32
            )
            * weight_scale
        ).astype(jnp.bfloat16),
        "dp",
        scatter_dimension=0,
        tiled=True,
    )
    weight_grad = lax.psum(rows_here, "seq").astype(jnp.float32)
    return (grads[None], weight_grad)


def dot(a, b, a_dim=1, b_dim=0):
    return lax.dot_general(a, b, (((a_dim,), (b_dim,)), ((), ())), preferred_element_type=F32)


def cols(h):
    return slice(h * HS, (h + 1) * HS)


def vmem():
    return pl.BlockSpec(memory_space=pltpu.VMEM)


def smem():
    return pl.BlockSpec(memory_space=pltpu.SMEM)


def params(mebibytes):
    return pltpu.CompilerParams(vmem_limit_bytes=mebibytes << 20)


def hbm():
    return pl.BlockSpec(memory_space=pltpu.HBM)


def state_kernel(meta, q, k, v, g, send, held, sems):
    copies = [
        pltpu.make_async_copy(ref, held.at[i], sems.at[i]) for i, ref in enumerate((q, k, v, g))
    ]
    for copy in copies:
        copy.start()
    for copy in copies:
        copy.wait()
    upper = meta[1] == 1
    for h in range(HEADS):
        left = jnp.where(upper, held[0, :, cols(h)], held[1, :, cols(h)])
        right = jnp.where(upper, held[3, :, cols(h)], held[2, :, cols(h)])
        send[h] = dot(left, right, 0, 0).astype(BF16)


def local_kernel(x, mine, other, local, turned, states, x0, sem):
    copy = pltpu.make_async_copy(x, x0, sem)
    copy.start()
    count = mine.shape[1]
    row = lax.broadcasted_iota(jnp.int32, (count, count), 0)
    col = lax.broadcasted_iota(jnp.int32, (count, count), 1)
    causal = row >= col
    causal_turned = row <= col
    for b, (q, k, v, g) in enumerate(tuple(ref.at[i] for i in range(4)) for ref in (mine, other)):
        for h in range(HEADS):
            qh, kh, vh, gh = (ref[:, cols(h)] for ref in (q, k, v, g))
            qt, kt, vt, gt = qh.T, kh.T, vh.T, gh.T
            a_turned = jnp.where(causal_turned, dot(vh, gt), 0.0).astype(BF16)
            a = jnp.where(causal, dot(gh, vt), 0.0).astype(BF16)
            s = jnp.where(causal, dot(qh, kt), 0.0).astype(BF16)
            local[b, 0, cols(h)] = dot(kt, a_turned)
            local[b, 1, cols(h)] = dot(qt, a)
            local[b, 2, cols(h)] = dot(gt, s)
            states[b, 0, h] = dot(kt, vh).astype(BF16)
            states[b, 1, h] = dot(qt, gh).astype(BF16)
            turned[b, 0, h] = gt
            turned[b, 1, h] = vt
            turned[b, 2, h] = kt
    copy.wait()


def column(table, i):
    return pl.ds(pl.multiple_of(table[4 + i] * BLOCK, BLOCK), BLOCK)


def weights(table, first, grads, x0, x1, out):
    for i in range(0, 8, 2):
        x = jnp.concatenate(
            [
                jnp.concatenate([ref[:, column(table, first + i + j)] for j in range(2)], axis=1)
                for ref in (x0, x1)
            ],
            axis=0,
        )
        total = dot(grads, x)
        out[i] = total[:, :BLOCK].astype(BF16)
        out[i + 1] = total[:, BLOCK:].astype(BF16)


def first_kernel(meta, local, turned, states, near, far, x0, x1, grads, out, *, scale):
    core = meta[0].astype(F32)
    upper = meta[1].astype(F32)
    width = HEADS * HS
    tokens = x0.shape[0]
    for h in range(HEADS):
        outside = near[h].astype(F32) + far[h].astype(F32)
        before = outside * upper
        after = outside * (1.0 - upper)
        for b in range(2):
            late = core if b == 0 else 1.0 - core
            prefix = (before + states[1 - b, 0, h].astype(F32) * late).astype(BF16)
            suffix = (after + states[1 - b, 1, h].astype(F32) * (1.0 - late)).astype(BF16)
            extra = (
                dot(prefix, turned[b, 0, h]),
                dot(suffix, turned[b, 1, h]),
                dot(suffix, turned[b, 2, h], 0, 0),
            )
            for part in range(3):
                total = (local[b, part, cols(h)] + extra[part]) * scale
                rows = slice(part * width + h * HS, part * width + (h + 1) * HS)
                grads[rows, b * tokens : (b + 1) * tokens] = total.astype(BF16)
    weights(meta, 8, grads[:width], x0, x1, out)


def other_kernel(meta, grads, x0, x1, out, *, part):
    width = HEADS * HS
    weights(meta, 16 * part + 8, grads[part * width : (part + 1) * width], x0, x1, out)


def keep_kernel(meta, grads, x0, x1, out_0, out_1, out_2, own):
    width = HEADS * HS
    for part, out in enumerate((out_0, out_1, out_2)):
        weights(meta, 16 * part, grads[part * width : (part + 1) * width], x0, x1, out)
    for i in range(0, grads.shape[0], HS):
        own[:, i : i + HS] = grads[i : i + HS, : own.shape[0]].T


def place_kernel(meta, *refs):
    out = refs[-1]
    column = 0
    for part in range(0, len(refs) - 1, 4):
        for turn, block in zip((0, 2, 1, 3), refs[part : part + 4]):
            rows = pl.ds(pl.multiple_of((meta[2] ^ turn) * BLOCK, BLOCK), BLOCK)
            out[rows, column : column + block.shape[1]] = block[...].astype(F32)
        column += refs[part].shape[1]


def final_kernel(total, here, out, *, scale):
    out[...] = ((total[0] + here[0].astype(F32)) * scale).T.astype(BF16)


def after(value, *others):
    return lax.optimization_barrier((value, *others))[0]


def partners(core0, core1, seq_count, dp_count):
    pairs = []
    for s in range(seq_count):
        for d in range(dp_count):
            ds, dd = (core0, core1)[s % 2]
            pairs.append((s * dp_count + d, (s ^ ds) * dp_count + (d ^ dd)))
    return pairs


def on_device(inputs, queries, keys, values, out_grad):
    tokens = queries.shape[1]
    seq_count = lax.axis_size("seq")
    dp_count = lax.axis_size("dp")
    length_all = tokens * seq_count
    scale = float(1.0 / (HS * length_all) ** 0.5)
    weight_scale = float(1.0 / (dp_count * length_all) ** 0.5)
    features = inputs[0]
    blocks = [value[0] for value in (queries, keys, values, out_grad)]
    stay = lambda value: pltpu.with_memory_space_constraint(value, pltpu.HBM)
    width = blocks[0].shape[1]
    rows = features.shape[1] // (seq_count * dp_count)

    swap = lambda value, core0, core1: lax.ppermute(
        value, AXES, partners(core0, core1, seq_count, dp_count)
    )
    sibling, across, y, z1, z2 = (1, 0), (2, 0), (0, 1), (0, 2), (0, 4)

    s, d = lax.axis_index("seq"), lax.axis_index("dp")
    core, upper = s & 1, s >> 1
    orders = (
        ((across, y), (y, across), (z1, z1), (z2, z2)),
        ((across, y), (y, across), (z1, z1), (z2, z2)),
        ((z1, z1), (across, y), (y, across), (z2, z2)),
    )
    lane = jnp.arange(4 + 16 * len(orders), dtype=jnp.int32)
    bits = lane - 4
    spot = jnp.zeros_like(lane)
    for part, order in enumerate(orders):
        for i, way in enumerate(order):
            bit = (bits >> (3 - i)) & 1
            jump = [ds | dd * seq_count for ds, dd in way]
            flip = bit * jnp.where(core == 0, jump[0], jump[1])
            spot = spot ^ jnp.where(bits >> 4 == part, flip, 0)
    spot = spot ^ (d * seq_count + s)
    meta = jnp.where(
        lane == 0, core, jnp.where(lane == 1, upper, jnp.where(lane == 2, s, spot))
    ).astype(jnp.int32)

    send, mine = pl.pallas_call(
        state_kernel,
        in_specs=[smem()] + [hbm()] * 4,
        out_specs=[vmem()] * 2,
        out_shape=[
            jax.ShapeDtypeStruct((HEADS, HS, HS), BF16),
            jax.ShapeDtypeStruct((4, tokens, width), BF16),
        ],
        scratch_shapes=[pltpu.SemaphoreType.DMA((4,))],
        compiler_params=params(4),
    )(meta, *map(stay, blocks))
    near = swap(send, across, across)
    other = swap(mine, sibling, sibling)
    other_x = swap(features, sibling, sibling)

    local, turned, states, mine_x = pl.pallas_call(
        local_kernel,
        in_specs=[hbm()] + [vmem()] * 2,
        out_specs=[vmem()] * 4,
        out_shape=[
            jax.ShapeDtypeStruct((2, 3, width, tokens), F32),
            jax.ShapeDtypeStruct((2, 3, HEADS, HS, tokens), BF16),
            jax.ShapeDtypeStruct((2, 2, HEADS, HS, HS), BF16),
            jax.ShapeDtypeStruct(features.shape, BF16),
        ],
        scratch_shapes=[pltpu.SemaphoreType.DMA],
        compiler_params=params(16),
    )(stay(features), mine, other)
    near = after(near, states)
    far = swap(near, sibling, sibling)
    half = jax.ShapeDtypeStruct((8, width, BLOCK), BF16)
    grads, going = pl.pallas_call(
        functools.partial(first_kernel, scale=scale),
        in_specs=[smem()] + [vmem()] * 7,
        out_specs=[vmem()] * 2,
        out_shape=[jax.ShapeDtypeStruct((3 * width, 2 * tokens), BF16), half],
        compiler_params=params(16),
    )(meta, local, turned, states, near, far, mine_x, other_x)
    here = [swap(going, *orders[0][0]), None, None]
    for part in (2, 1):
        going = pl.pallas_call(
            functools.partial(other_kernel, part=part),
            in_specs=[smem()] + [vmem()] * 3,
            out_specs=vmem(),
            out_shape=half,
            compiler_params=params(16),
        )(meta, after(grads, going), mine_x, other_x)
        here[part] = swap(going, *orders[part][0])
    *kept, own = pl.pallas_call(
        keep_kernel,
        in_specs=[smem()] + [vmem()] * 3,
        out_specs=[vmem()] * 4,
        out_shape=[half] * 3 + [jax.ShapeDtypeStruct((tokens, 3 * width), BF16)],
        compiler_params=params(16),
    )(meta, after(grads, going), mine_x, other_x)

    def step(kept, here, way):
        count = kept.shape[0] // 2
        total = kept.astype(F32) + here.astype(F32)
        going = total[count:].astype(BF16)
        return total[:count], going, swap(going, *way)

    def finish(kept, here):
        final = pl.pallas_call(
            functools.partial(final_kernel, scale=weight_scale),
            in_specs=[vmem()] * 2,
            out_specs=vmem(),
            out_shape=jax.ShapeDtypeStruct((BLOCK, kept.shape[1]), BF16),
            compiler_params=params(4),
        )(kept, here)
        facing = swap(final, across, across)
        return final, facing, swap(final, sibling, sibling), swap(facing, sibling, sibling)

    latest = kept[0]
    for part, level in ((0, 1), (1, 1), (2, 1), (0, 2), (1, 2), (2, 2), (0, 3), (1, 3), (2, 3)):
        kept[part], latest, here[part] = step(
            kept[part], after(here[part], latest), orders[part][level]
        )
    parts = {}
    parts[0] = finish(kept[0], after(here[0], latest))
    parts[1] = finish(kept[1], after(here[1], parts[0][0]))
    parts[2] = finish(kept[2], after(here[2], parts[1][0], parts[0][1]))
    weight_grad = pl.pallas_call(
        place_kernel,
        in_specs=[smem()] + [vmem()] * 12,
        out_specs=vmem(),
        out_shape=jax.ShapeDtypeStruct((seq_count * rows, 3 * width), F32),
        compiler_params=params(8),
    )(meta, *parts[0], *parts[1], *parts[2])
    return (own[None], weight_grad)


def solution(mesh):
    in_specs = (
        P("dp", "seq", None),
        P("dp", "seq", None),
        P("dp", "seq", None),
        P("dp", "seq", None),
        P("dp", "seq", None),
    )
    out_specs = (P("dp", "seq", None), P("dp", None))
    fast = mesh.shape["seq"] == 4 and mesh.shape["dp"] == 8
    body = on_device if fast else on_device_any
    return jax.shard_map(
        body, mesh=mesh, in_specs=in_specs, out_specs=out_specs, check_vma=False
    )
```

```python
import functools

import jax
import jax.numpy as jnp
from jax import lax
from jax.experimental import pallas as pl
from jax.experimental.pallas import tpu as pltpu
from jax.sharding import PartitionSpec as P

HS = 128
HEADS = 2
BLOCK = 128
BF16 = jnp.bfloat16
F32 = jnp.float32
AXES = ("seq", "dp")


def block_grads(query, key, value, grad_out, prefix, suffix, scale):
    count = query.shape[0]
    causal = jnp.arange(count)[:, None] >= jnp.arange(count)[None, :]
    f32 = jnp.float32
    score_a = jnp.einsum("thd,shd->hts", grad_out, value, preferred_element_type=f32)
    score_a = jnp.where(causal[None], score_a, 0.0).astype(jnp.bfloat16)
    score_b = jnp.einsum("thd,shd->hts", query, key, preferred_element_type=f32)
    score_b = jnp.where(causal[None], score_b, 0.0).astype(jnp.bfloat16)
    grad_q = jnp.einsum("hts,shd->thd", score_a, key, preferred_element_type=f32) + jnp.einsum(
        "thb,hab->tha", grad_out, prefix, preferred_element_type=f32
    )
    grad_k = jnp.einsum("htj,thd->jhd", score_a, query, preferred_element_type=f32) + jnp.einsum(
        "jhb,hab->jha", value, suffix, preferred_element_type=f32
    )
    grad_v = jnp.einsum("htj,thd->jhd", score_b, grad_out, preferred_element_type=f32) + jnp.einsum(
        "jha,hab->jhb", key, suffix, preferred_element_type=f32
    )
    joined = jnp.concatenate([grad_q, grad_k, grad_v], axis=1) * scale
    return joined.reshape(count, -1).astype(jnp.bfloat16)


def on_device_any(inputs, queries, keys, values, out_grad):
    tokens = queries.shape[1]
    seq_count = lax.axis_size("seq")
    batch_count = lax.axis_size("dp")
    length_all = tokens * seq_count
    scale = 1.0 / jnp.sqrt(jnp.float32(HS * length_all))
    weight_scale = 1.0 / jnp.sqrt(jnp.float32(batch_count * length_all))
    shape = (tokens, HEADS, HS)
    query = queries[0].reshape(shape)
    key = keys[0].reshape(shape)
    value = values[0].reshape(shape)
    grad_out = out_grad[0].reshape(shape)
    kv_state = jnp.einsum("lhi,lhj->hij", key, value, preferred_element_type=jnp.float32).astype(
        jnp.bfloat16
    )
    dq_state = jnp.einsum(
        "lhi,lhj->hij", query, grad_out, preferred_element_type=jnp.float32
    ).astype(jnp.bfloat16)
    stacked = jnp.stack([kv_state, dq_state])[None]
    position = lax.axis_index("seq")
    piece = lax.all_gather(stacked, "seq", axis=0, tiled=True)
    owners = jnp.arange(piece.shape[0])
    lower = (owners < position).astype(jnp.float32)
    higher = (owners > position).astype(jnp.float32)
    wide = piece.astype(jnp.float32)
    prefix = jnp.einsum("n,nhij->hij", lower, wide[:, 0])
    suffix = jnp.einsum("n,nhij->hij", higher, wide[:, 1])
    prefix = prefix.astype(jnp.bfloat16)
    suffix = suffix.astype(jnp.bfloat16)
    grads = block_grads(query, key, value, grad_out, prefix, suffix, scale)
    features = inputs[0]
    rows_here = lax.psum_scatter(
        (
            lax.dot_general(
                features, grads, (((0,), (0,)), ((), ())), preferred_element_type=jnp.float32
            )
            * weight_scale
        ).astype(jnp.bfloat16),
        "dp",
        scatter_dimension=0,
        tiled=True,
    )
    weight_grad = lax.psum(rows_here, "seq").astype(jnp.float32)
    return (grads[None], weight_grad)


def dot(a, b, a_dim=1, b_dim=0):
    return lax.dot_general(a, b, (((a_dim,), (b_dim,)), ((), ())), preferred_element_type=F32)


def cols(h):
    return slice(h * HS, (h + 1) * HS)


def vmem():
    return pl.BlockSpec(memory_space=pltpu.VMEM)


def smem():
    return pl.BlockSpec(memory_space=pltpu.SMEM)


def params(mebibytes):
    return pltpu.CompilerParams(vmem_limit_bytes=mebibytes << 20)


def hbm():
    return pl.BlockSpec(memory_space=pltpu.HBM)


def state_kernel(meta, q, k, v, g, send, held, sems):
    copies = [
        pltpu.make_async_copy(ref, held.at[i], sems.at[i]) for i, ref in enumerate((q, k, v, g))
    ]
    for copy in copies:
        copy.start()
    for copy in copies:
        copy.wait()
    upper = meta[1] == 1
    for h in range(HEADS):
        left = jnp.where(upper, held[0, :, cols(h)], held[1, :, cols(h)])
        right = jnp.where(upper, held[3, :, cols(h)], held[2, :, cols(h)])
        send[h] = dot(left, right, 0, 0).astype(BF16)


def local_kernel(x, mine, other, local, turned, states, x0, sem):
    copy = pltpu.make_async_copy(x, x0, sem)
    copy.start()
    count = mine.shape[1]
    row = lax.broadcasted_iota(jnp.int32, (count, count), 0)
    col = lax.broadcasted_iota(jnp.int32, (count, count), 1)
    causal = row >= col
    causal_turned = row <= col
    for b, (q, k, v, g) in enumerate(tuple(ref.at[i] for i in range(4)) for ref in (mine, other)):
        for h in range(HEADS):
            qh, kh, vh, gh = (ref[:, cols(h)] for ref in (q, k, v, g))
            qt, kt, vt, gt = qh.T, kh.T, vh.T, gh.T
            a_turned = jnp.where(causal_turned, dot(vh, gt), 0.0).astype(BF16)
            a = jnp.where(causal, dot(gh, vt), 0.0).astype(BF16)
            s = jnp.where(causal, dot(qh, kt), 0.0).astype(BF16)
            local[b, 0, cols(h)] = dot(kt, a_turned)
            local[b, 1, cols(h)] = dot(qt, a)
            local[b, 2, cols(h)] = dot(gt, s)
            states[b, 0, h] = dot(kt, vh).astype(BF16)
            states[b, 1, h] = dot(qt, gh).astype(BF16)
            turned[b, 0, h] = gt
            turned[b, 1, h] = vt
            turned[b, 2, h] = kt
    copy.wait()


def column(table, i):
    return pl.ds(pl.multiple_of(table[4 + i] * BLOCK, BLOCK), BLOCK)


def weights(table, first, grads, x0, x1, out):
    for i in range(0, 8, 2):
        x = jnp.concatenate(
            [
                jnp.concatenate([ref[:, column(table, first + i + j)] for j in range(2)], axis=1)
                for ref in (x0, x1)
            ],
            axis=0,
        )
        total = dot(grads, x)
        out[i] = total[:, :BLOCK].astype(BF16)
        out[i + 1] = total[:, BLOCK:].astype(BF16)


def first_kernel(meta, local, turned, states, near, far, x0, x1, grads, out, *, scale):
    core = meta[0].astype(F32)
    upper = meta[1].astype(F32)
    width = HEADS * HS
    tokens = x0.shape[0]
    for h in range(HEADS):
        outside = near[h].astype(F32) + far[h].astype(F32)
        before = outside * upper
        after = outside * (1.0 - upper)
        for b in range(2):
            late = core if b == 0 else 1.0 - core
            prefix = (before + states[1 - b, 0, h].astype(F32) * late).astype(BF16)
            suffix = (after + states[1 - b, 1, h].astype(F32) * (1.0 - late)).astype(BF16)
            extra = (
                dot(prefix, turned[b, 0, h]),
                dot(suffix, turned[b, 1, h]),
                dot(suffix, turned[b, 2, h], 0, 0),
            )
            for part in range(3):
                total = (local[b, part, cols(h)] + extra[part]) * scale
                rows = slice(part * width + h * HS, part * width + (h + 1) * HS)
                grads[rows, b * tokens : (b + 1) * tokens] = total.astype(BF16)
    weights(meta, 8, grads[:width], x0, x1, out)


def other_kernel(meta, grads, x0, x1, out, *, part):
    width = HEADS * HS
    weights(meta, 16 * part + 8, grads[part * width : (part + 1) * width], x0, x1, out)


def keep_kernel(meta, grads, x0, x1, out_0, out_1, out_2, own):
    width = HEADS * HS
    for part, out in enumerate((out_0, out_1, out_2)):
        weights(meta, 16 * part, grads[part * width : (part + 1) * width], x0, x1, out)
    for i in range(0, grads.shape[0], HS):
        own[:, i : i + HS] = grads[i : i + HS, : own.shape[0]].T


def place_kernel(meta, *refs, parts, first):
    out, wide, sems = refs[-3:]
    copies = []
    size = wide.shape[3]
    for part in range(parts):
        columns = pl.ds((first + part) * size, size)
        for i, (turn, block) in enumerate(zip((0, 2, 1, 3), refs[4 * part : 4 * part + 4])):
            wide[part, i] = block[...].astype(F32)
            rows = pl.ds(pl.multiple_of((meta[2] ^ turn) * BLOCK, BLOCK), BLOCK)
            copy = pltpu.make_async_copy(wide.at[part, i], out.at[rows, columns], sems.at[part, i])
            copy.start()
            copies.append(copy)
    for copy in copies:
        copy.wait()


def place(meta, blocks, first, shape, before=()):
    parts = len(blocks) // 4
    return pl.pallas_call(
        functools.partial(place_kernel, parts=parts, first=first),
        in_specs=[smem()] + [vmem()] * len(blocks) + [hbm()] * len(before),
        out_specs=hbm(),
        out_shape=jax.ShapeDtypeStruct(shape, F32),
        scratch_shapes=[
            pltpu.VMEM((parts, 4, *blocks[0].shape), F32),
            pltpu.SemaphoreType.DMA((parts, 4)),
        ],
        input_output_aliases={len(blocks) + 1: 0} if before else {},
        compiler_params=params(8),
    )(meta, *blocks, *before)


def final_kernel(total, here, out, *, scale):
    out[...] = ((total[0] + here[0].astype(F32)) * scale).T.astype(BF16)


def after(value, *others):
    return lax.optimization_barrier((value, *others))[0]


def partners(core0, core1, seq_count, dp_count):
    pairs = []
    for s in range(seq_count):
        for d in range(dp_count):
            ds, dd = (core0, core1)[s % 2]
            pairs.append((s * dp_count + d, (s ^ ds) * dp_count + (d ^ dd)))
    return pairs


def on_device(inputs, queries, keys, values, out_grad):
    tokens = queries.shape[1]
    seq_count = lax.axis_size("seq")
    dp_count = lax.axis_size("dp")
    length_all = tokens * seq_count
    scale = float(1.0 / (HS * length_all) ** 0.5)
    weight_scale = float(1.0 / (dp_count * length_all) ** 0.5)
    features = inputs[0]
    blocks = [value[0] for value in (queries, keys, values, out_grad)]
    stay = lambda value: pltpu.with_memory_space_constraint(value, pltpu.HBM)
    width = blocks[0].shape[1]
    rows = features.shape[1] // (seq_count * dp_count)

    swap = lambda value, core0, core1: lax.ppermute(
        value, AXES, partners(core0, core1, seq_count, dp_count)
    )
    sibling, across, y, z1, z2 = (1, 0), (2, 0), (0, 1), (0, 2), (0, 4)

    s, d = lax.axis_index("seq"), lax.axis_index("dp")
    core, upper = s & 1, s >> 1
    orders = (
        ((across, y), (y, z1), (z1, across), (z2, z2)),
        ((across, y), (y, across), (z1, z1), (z2, z2)),
        ((z1, z1), (y, across), (across, y), (z2, z2)),
    )
    lane = jnp.arange(4 + 16 * len(orders), dtype=jnp.int32)
    bits = lane - 4
    spot = jnp.zeros_like(lane)
    for part, order in enumerate(orders):
        for i, way in enumerate(order):
            bit = (bits >> (3 - i)) & 1
            jump = [ds | dd * seq_count for ds, dd in way]
            flip = bit * jnp.where(core == 0, jump[0], jump[1])
            spot = spot ^ jnp.where(bits >> 4 == part, flip, 0)
    spot = spot ^ (d * seq_count + s)
    meta = jnp.where(
        lane == 0, core, jnp.where(lane == 1, upper, jnp.where(lane == 2, s, spot))
    ).astype(jnp.int32)

    send, mine = pl.pallas_call(
        state_kernel,
        in_specs=[smem()] + [hbm()] * 4,
        out_specs=[vmem()] * 2,
        out_shape=[
            jax.ShapeDtypeStruct((HEADS, HS, HS), BF16),
            jax.ShapeDtypeStruct((4, tokens, width), BF16),
        ],
        scratch_shapes=[pltpu.SemaphoreType.DMA((4,))],
        compiler_params=params(4),
    )(meta, *map(stay, blocks))
    near = swap(send, across, across)
    other = swap(mine, sibling, sibling)
    other_x = swap(features, sibling, sibling)

    local, turned, states, mine_x = pl.pallas_call(
        local_kernel,
        in_specs=[hbm()] + [vmem()] * 2,
        out_specs=[vmem()] * 4,
        out_shape=[
            jax.ShapeDtypeStruct((2, 3, width, tokens), F32),
            jax.ShapeDtypeStruct((2, 3, HEADS, HS, tokens), BF16),
            jax.ShapeDtypeStruct((2, 2, HEADS, HS, HS), BF16),
            jax.ShapeDtypeStruct(features.shape, BF16),
        ],
        scratch_shapes=[pltpu.SemaphoreType.DMA],
        compiler_params=params(16),
    )(stay(features), mine, other)
    near = after(near, states)
    far = swap(near, sibling, sibling)
    half = jax.ShapeDtypeStruct((8, width, BLOCK), BF16)
    grads, going = pl.pallas_call(
        functools.partial(first_kernel, scale=scale),
        in_specs=[smem()] + [vmem()] * 7,
        out_specs=[vmem()] * 2,
        out_shape=[jax.ShapeDtypeStruct((3 * width, 2 * tokens), BF16), half],
        compiler_params=params(16),
    )(meta, local, turned, states, near, far, mine_x, other_x)
    here = [swap(going, *orders[0][0]), None, None]
    for part in (2, 1):
        going = pl.pallas_call(
            functools.partial(other_kernel, part=part),
            in_specs=[smem()] + [vmem()] * 3,
            out_specs=vmem(),
            out_shape=half,
            compiler_params=params(16),
        )(meta, after(grads, going), mine_x, other_x)
        here[part] = swap(going, *orders[part][0])
    *kept, own = pl.pallas_call(
        keep_kernel,
        in_specs=[smem()] + [vmem()] * 3,
        out_specs=[vmem()] * 4,
        out_shape=[half] * 3 + [jax.ShapeDtypeStruct((tokens, 3 * width), BF16)],
        compiler_params=params(16),
    )(meta, after(grads, going), mine_x, other_x)

    def step(kept, here, way):
        count = kept.shape[0] // 2
        total = kept.astype(F32) + here.astype(F32)
        going = total[count:].astype(BF16)
        return total[:count], going, swap(going, *way)

    def finish(kept, here):
        final = pl.pallas_call(
            functools.partial(final_kernel, scale=weight_scale),
            in_specs=[vmem()] * 2,
            out_specs=vmem(),
            out_shape=jax.ShapeDtypeStruct((BLOCK, kept.shape[1]), BF16),
            compiler_params=params(4),
        )(kept, here)
        facing = swap(final, across, across)
        return final, facing, swap(final, sibling, sibling), swap(facing, sibling, sibling)

    latest = kept[0]
    for part, level in ((0, 1), (1, 1), (2, 1), (0, 2), (1, 2), (2, 2), (0, 3), (1, 3), (2, 3)):
        kept[part], latest, here[part] = step(
            kept[part], after(here[part], latest), orders[part][level]
        )
    parts = {}
    parts[0] = finish(kept[0], after(here[0], latest))
    parts[1] = finish(kept[1], after(here[1], parts[0][0]))
    parts[2] = finish(kept[2], after(here[2], parts[1][0], parts[0][1]))
    shape = (seq_count * rows, 3 * width)
    weight_grad = place(meta, parts[0] + parts[1] + parts[2], 0, shape)
    return (own[None], weight_grad)


def solution(mesh):
    in_specs = (
        P("dp", "seq", None),
        P("dp", "seq", None),
        P("dp", "seq", None),
        P("dp", "seq", None),
        P("dp", "seq", None),
    )
    out_specs = (P("dp", "seq", None), P("dp", None))
    fast = mesh.shape["seq"] == 4 and mesh.shape["dp"] == 8
    body = on_device if fast else on_device_any
    return jax.shard_map(
        body, mesh=mesh, in_specs=in_specs, out_specs=out_specs, check_vma=False
    )
```

```python
import functools

import jax
import jax.numpy as jnp
from jax import lax
from jax.experimental import pallas as pl
from jax.experimental.pallas import tpu as pltpu
from jax.sharding import PartitionSpec as P

HS = 128
HEADS = 2
BLOCK = 128
BF16 = jnp.bfloat16
F32 = jnp.float32
AXES = ("seq", "dp")


def block_grads(query, key, value, grad_out, prefix, suffix, scale):
    count = query.shape[0]
    causal = jnp.arange(count)[:, None] >= jnp.arange(count)[None, :]
    f32 = jnp.float32
    score_a = jnp.einsum("thd,shd->hts", grad_out, value, preferred_element_type=f32)
    score_a = jnp.where(causal[None], score_a, 0.0).astype(jnp.bfloat16)
    score_b = jnp.einsum("thd,shd->hts", query, key, preferred_element_type=f32)
    score_b = jnp.where(causal[None], score_b, 0.0).astype(jnp.bfloat16)
    grad_q = jnp.einsum("hts,shd->thd", score_a, key, preferred_element_type=f32) + jnp.einsum(
        "thb,hab->tha", grad_out, prefix, preferred_element_type=f32
    )
    grad_k = jnp.einsum("htj,thd->jhd", score_a, query, preferred_element_type=f32) + jnp.einsum(
        "jhb,hab->jha", value, suffix, preferred_element_type=f32
    )
    grad_v = jnp.einsum("htj,thd->jhd", score_b, grad_out, preferred_element_type=f32) + jnp.einsum(
        "jha,hab->jhb", key, suffix, preferred_element_type=f32
    )
    joined = jnp.concatenate([grad_q, grad_k, grad_v], axis=1) * scale
    return joined.reshape(count, -1).astype(jnp.bfloat16)


def on_device_any(inputs, queries, keys, values, out_grad):
    tokens = queries.shape[1]
    seq_count = lax.axis_size("seq")
    batch_count = lax.axis_size("dp")
    length_all = tokens * seq_count
    scale = 1.0 / jnp.sqrt(jnp.float32(HS * length_all))
    weight_scale = 1.0 / jnp.sqrt(jnp.float32(batch_count * length_all))
    shape = (tokens, HEADS, HS)
    query = queries[0].reshape(shape)
    key = keys[0].reshape(shape)
    value = values[0].reshape(shape)
    grad_out = out_grad[0].reshape(shape)
    kv_state = jnp.einsum("lhi,lhj->hij", key, value, preferred_element_type=jnp.float32).astype(
        jnp.bfloat16
    )
    dq_state = jnp.einsum(
        "lhi,lhj->hij", query, grad_out, preferred_element_type=jnp.float32
    ).astype(jnp.bfloat16)
    stacked = jnp.stack([kv_state, dq_state])[None]
    position = lax.axis_index("seq")
    piece = lax.all_gather(stacked, "seq", axis=0, tiled=True)
    owners = jnp.arange(piece.shape[0])
    lower = (owners < position).astype(jnp.float32)
    higher = (owners > position).astype(jnp.float32)
    wide = piece.astype(jnp.float32)
    prefix = jnp.einsum("n,nhij->hij", lower, wide[:, 0])
    suffix = jnp.einsum("n,nhij->hij", higher, wide[:, 1])
    prefix = prefix.astype(jnp.bfloat16)
    suffix = suffix.astype(jnp.bfloat16)
    grads = block_grads(query, key, value, grad_out, prefix, suffix, scale)
    features = inputs[0]
    rows_here = lax.psum_scatter(
        (
            lax.dot_general(
                features, grads, (((0,), (0,)), ((), ())), preferred_element_type=jnp.float32
            )
            * weight_scale
        ).astype(jnp.bfloat16),
        "dp",
        scatter_dimension=0,
        tiled=True,
    )
    weight_grad = lax.psum(rows_here, "seq").astype(jnp.float32)
    return (grads[None], weight_grad)


def dot(a, b, a_dim=1, b_dim=0):
    return lax.dot_general(a, b, (((a_dim,), (b_dim,)), ((), ())), preferred_element_type=F32)


def cols(h):
    return slice(h * HS, (h + 1) * HS)


def vmem():
    return pl.BlockSpec(memory_space=pltpu.VMEM)


def smem():
    return pl.BlockSpec(memory_space=pltpu.SMEM)


def params(mebibytes):
    return pltpu.CompilerParams(vmem_limit_bytes=mebibytes << 20)


def hbm():
    return pl.BlockSpec(memory_space=pltpu.HBM)


def state_kernel(meta, q, k, v, g, send, held, sems):
    copies = [
        pltpu.make_async_copy(ref, held.at[i], sems.at[i]) for i, ref in enumerate((q, k, v, g))
    ]
    for copy in copies:
        copy.start()
    for copy in copies:
        copy.wait()
    upper = meta[1] == 1
    for h in range(HEADS):
        left = jnp.where(upper, held[0, :, cols(h)], held[1, :, cols(h)])
        right = jnp.where(upper, held[3, :, cols(h)], held[2, :, cols(h)])
        send[h] = dot(left, right, 0, 0).astype(BF16)


def local_kernel(x, mine, other, local, turned, states, x0, sem):
    copy = pltpu.make_async_copy(x, x0, sem)
    copy.start()
    count = mine.shape[1]
    row = lax.broadcasted_iota(jnp.int32, (count, count), 0)
    col = lax.broadcasted_iota(jnp.int32, (count, count), 1)
    causal = row >= col
    causal_turned = row <= col
    for b, (q, k, v, g) in enumerate(tuple(ref.at[i] for i in range(4)) for ref in (mine, other)):
        for h in range(HEADS):
            qh, kh, vh, gh = (ref[:, cols(h)] for ref in (q, k, v, g))
            qt, kt, vt, gt = qh.T, kh.T, vh.T, gh.T
            a_turned = jnp.where(causal_turned, dot(vh, gt), 0.0).astype(BF16)
            a = jnp.where(causal, dot(gh, vt), 0.0).astype(BF16)
            s = jnp.where(causal, dot(qh, kt), 0.0).astype(BF16)
            local[b, 0, cols(h)] = dot(kt, a_turned)
            local[b, 1, cols(h)] = dot(qt, a)
            local[b, 2, cols(h)] = dot(gt, s)
            states[b, 0, h] = dot(kt, vh).astype(BF16)
            states[b, 1, h] = dot(qt, gh).astype(BF16)
            turned[b, 0, h] = gt
            turned[b, 1, h] = vt
            turned[b, 2, h] = kt
    copy.wait()


def column(table, i):
    return pl.ds(pl.multiple_of(table[4 + i] * BLOCK, BLOCK), BLOCK)


def weights(table, first, grads, x0, x1, out):
    for i in range(0, 8, 2):
        x = jnp.concatenate(
            [
                jnp.concatenate([ref[:, column(table, first + i + j)] for j in range(2)], axis=1)
                for ref in (x0, x1)
            ],
            axis=0,
        )
        total = dot(grads, x)
        out[i] = total[:, :BLOCK].astype(BF16)
        out[i + 1] = total[:, BLOCK:].astype(BF16)


def first_kernel(meta, local, turned, states, near, far, x0, x1, grads, out, *, scale):
    core = meta[0].astype(F32)
    upper = meta[1].astype(F32)
    width = HEADS * HS
    tokens = x0.shape[0]
    for h in range(HEADS):
        outside = near[h].astype(F32) + far[h].astype(F32)
        before = outside * upper
        after = outside * (1.0 - upper)
        for b in range(2):
            late = core if b == 0 else 1.0 - core
            prefix = (before + states[1 - b, 0, h].astype(F32) * late).astype(BF16)
            suffix = (after + states[1 - b, 1, h].astype(F32) * (1.0 - late)).astype(BF16)
            extra = (
                dot(prefix, turned[b, 0, h]),
                dot(suffix, turned[b, 1, h]),
                dot(suffix, turned[b, 2, h], 0, 0),
            )
            for part in range(3):
                total = (local[b, part, cols(h)] + extra[part]) * scale
                rows = slice(part * width + h * HS, part * width + (h + 1) * HS)
                grads[rows, b * tokens : (b + 1) * tokens] = total.astype(BF16)
    weights(meta, 8, grads[:width], x0, x1, out)


def other_kernel(meta, grads, x0, x1, out, *, part):
    width = HEADS * HS
    weights(meta, 16 * part + 8, grads[part * width : (part + 1) * width], x0, x1, out)


def keep_kernel(meta, grads, x0, x1, out_0, out_1, out_2, own):
    width = HEADS * HS
    for part, out in enumerate((out_0, out_1, out_2)):
        weights(meta, 16 * part, grads[part * width : (part + 1) * width], x0, x1, out)
    for i in range(0, grads.shape[0], HS):
        own[:, i : i + HS] = grads[i : i + HS, : own.shape[0]].T


def place_kernel(meta, *refs, parts, first):
    out, wide, sems = refs[-3:]
    copies = []
    size = wide.shape[3]
    for part in range(parts):
        columns = pl.ds((first + part) * size, size)
        for i, (turn, block) in enumerate(zip((0, 2, 1, 3), refs[4 * part : 4 * part + 4])):
            wide[part, i] = block[...].astype(F32)
            rows = pl.ds(pl.multiple_of((meta[2] ^ turn) * BLOCK, BLOCK), BLOCK)
            copy = pltpu.make_async_copy(wide.at[part, i], out.at[rows, columns], sems.at[part, i])
            copy.start()
            copies.append(copy)
    for copy in copies:
        copy.wait()


def place(meta, blocks, first, shape, before=()):
    parts = len(blocks) // 4
    return pl.pallas_call(
        functools.partial(place_kernel, parts=parts, first=first),
        in_specs=[smem()] + [vmem()] * len(blocks) + [hbm()] * len(before),
        out_specs=hbm(),
        out_shape=jax.ShapeDtypeStruct(shape, F32),
        scratch_shapes=[
            pltpu.VMEM((parts, 4, *blocks[0].shape), F32),
            pltpu.SemaphoreType.DMA((parts, 4)),
        ],
        input_output_aliases={len(blocks) + 1: 0} if before else {},
        compiler_params=params(8),
    )(meta, *blocks, *before)


def final_kernel(total, here, out, *, scale):
    out[...] = ((total[0] + here[0].astype(F32)) * scale).T.astype(BF16)


def after(value, *others):
    return lax.optimization_barrier((value, *others))[0]


def partners(core0, core1, seq_count, dp_count):
    pairs = []
    for s in range(seq_count):
        for d in range(dp_count):
            ds, dd = (core0, core1)[s % 2]
            pairs.append((s * dp_count + d, (s ^ ds) * dp_count + (d ^ dd)))
    return pairs


def on_device(inputs, queries, keys, values, out_grad):
    tokens = queries.shape[1]
    seq_count = lax.axis_size("seq")
    dp_count = lax.axis_size("dp")
    length_all = tokens * seq_count
    scale = float(1.0 / (HS * length_all) ** 0.5)
    weight_scale = float(1.0 / (dp_count * length_all) ** 0.5)
    features = inputs[0]
    blocks = [value[0] for value in (queries, keys, values, out_grad)]
    stay = lambda value: pltpu.with_memory_space_constraint(value, pltpu.HBM)
    width = blocks[0].shape[1]
    rows = features.shape[1] // (seq_count * dp_count)

    swap = lambda value, core0, core1: lax.ppermute(
        value, AXES, partners(core0, core1, seq_count, dp_count)
    )
    sibling, across, y, z1, z2 = (1, 0), (2, 0), (0, 1), (0, 2), (0, 4)

    s, d = lax.axis_index("seq"), lax.axis_index("dp")
    core, upper = s & 1, s >> 1
    orders = (
        ((across, y), (y, z1), (z1, across), (z2, z2)),
        ((across, y), (y, across), (z1, z1), (z2, z2)),
        ((z1, z1), (y, across), (across, y), (z2, z2)),
    )
    lane = jnp.arange(4 + 16 * len(orders), dtype=jnp.int32)
    bits = lane - 4
    spot = jnp.zeros_like(lane)
    for part, order in enumerate(orders):
        for i, way in enumerate(order):
            bit = (bits >> (3 - i)) & 1
            jump = [ds | dd * seq_count for ds, dd in way]
            flip = bit * jnp.where(core == 0, jump[0], jump[1])
            spot = spot ^ jnp.where(bits >> 4 == part, flip, 0)
    spot = spot ^ (d * seq_count + s)
    meta = jnp.where(
        lane == 0, core, jnp.where(lane == 1, upper, jnp.where(lane == 2, s, spot))
    ).astype(jnp.int32)

    send, mine = pl.pallas_call(
        state_kernel,
        in_specs=[smem()] + [hbm()] * 4,
        out_specs=[vmem()] * 2,
        out_shape=[
            jax.ShapeDtypeStruct((HEADS, HS, HS), BF16),
            jax.ShapeDtypeStruct((4, tokens, width), BF16),
        ],
        scratch_shapes=[pltpu.SemaphoreType.DMA((4,))],
        compiler_params=params(4),
    )(meta, *map(stay, blocks))
    near = swap(send, across, across)
    other = swap(mine, sibling, sibling)
    other_x = swap(features, sibling, sibling)

    local, turned, states, mine_x = pl.pallas_call(
        local_kernel,
        in_specs=[hbm()] + [vmem()] * 2,
        out_specs=[vmem()] * 4,
        out_shape=[
            jax.ShapeDtypeStruct((2, 3, width, tokens), F32),
            jax.ShapeDtypeStruct((2, 3, HEADS, HS, tokens), BF16),
            jax.ShapeDtypeStruct((2, 2, HEADS, HS, HS), BF16),
            jax.ShapeDtypeStruct(features.shape, BF16),
        ],
        scratch_shapes=[pltpu.SemaphoreType.DMA],
        compiler_params=params(16),
    )(stay(features), mine, other)
    near = after(near, states)
    far = swap(near, sibling, sibling)
    half = jax.ShapeDtypeStruct((8, width, BLOCK), BF16)
    grads, going = pl.pallas_call(
        functools.partial(first_kernel, scale=scale),
        in_specs=[smem()] + [vmem()] * 7,
        out_specs=[vmem()] * 2,
        out_shape=[jax.ShapeDtypeStruct((3 * width, 2 * tokens), BF16), half],
        compiler_params=params(16),
    )(meta, local, turned, states, near, far, mine_x, other_x)
    here = [swap(going, *orders[0][0]), None, None]
    for part in (2, 1):
        going = pl.pallas_call(
            functools.partial(other_kernel, part=part),
            in_specs=[smem()] + [vmem()] * 3,
            out_specs=vmem(),
            out_shape=half,
            compiler_params=params(16),
        )(meta, after(grads, going), mine_x, other_x)
        here[part] = swap(going, *orders[part][0])
    *kept, own = pl.pallas_call(
        keep_kernel,
        in_specs=[smem()] + [vmem()] * 3,
        out_specs=[vmem()] * 4,
        out_shape=[half] * 3 + [jax.ShapeDtypeStruct((tokens, 3 * width), BF16)],
        compiler_params=params(16),
    )(meta, after(grads, going), mine_x, other_x)

    def step(kept, here, way):
        count = kept.shape[0] // 2
        total = kept.astype(F32) + here.astype(F32)
        going = total[count:].astype(BF16)
        return total[:count], going, swap(going, *way)

    def finish(kept, here):
        final = pl.pallas_call(
            functools.partial(final_kernel, scale=weight_scale),
            in_specs=[vmem()] * 2,
            out_specs=vmem(),
            out_shape=jax.ShapeDtypeStruct((BLOCK, kept.shape[1]), BF16),
            compiler_params=params(4),
        )(kept, here)
        facing = swap(final, across, across)
        return final, facing, swap(final, sibling, sibling), swap(facing, sibling, sibling)

    latest = kept[0]
    for part, level in ((0, 1), (1, 1), (2, 1), (0, 2), (1, 2), (2, 2), (0, 3), (2, 3), (1, 3)):
        kept[part], latest, here[part] = step(
            kept[part], after(here[part], latest), orders[part][level]
        )
    parts = {}
    parts[0] = finish(kept[0], after(here[0], latest))
    parts[1] = finish(kept[1], after(here[1], parts[0][0]))
    parts[2] = finish(kept[2], after(here[2], parts[1][0], parts[0][1]))
    shape = (seq_count * rows, 3 * width)
    weight_grad = place(meta, parts[0] + parts[1] + parts[2], 0, shape)
    return (own[None], weight_grad)


def solution(mesh):
    in_specs = (
        P("dp", "seq", None),
        P("dp", "seq", None),
        P("dp", "seq", None),
        P("dp", "seq", None),
        P("dp", "seq", None),
    )
    out_specs = (P("dp", "seq", None), P("dp", None))
    fast = mesh.shape["seq"] == 4 and mesh.shape["dp"] == 8
    body = on_device if fast else on_device_any
    return jax.shard_map(
        body, mesh=mesh, in_specs=in_specs, out_specs=out_specs, check_vma=False
    )
```

```python
import functools

import jax
import jax.numpy as jnp
from jax import lax
from jax.experimental import pallas as pl
from jax.experimental.pallas import tpu as pltpu
from jax.sharding import PartitionSpec as P

HS = 128
HEADS = 2
BLOCK = 128
BF16 = jnp.bfloat16
F32 = jnp.float32
AXES = ("seq", "dp")


def block_grads(query, key, value, grad_out, prefix, suffix, scale):
    count = query.shape[0]
    causal = jnp.arange(count)[:, None] >= jnp.arange(count)[None, :]
    f32 = jnp.float32
    score_a = jnp.einsum("thd,shd->hts", grad_out, value, preferred_element_type=f32)
    score_a = jnp.where(causal[None], score_a, 0.0).astype(jnp.bfloat16)
    score_b = jnp.einsum("thd,shd->hts", query, key, preferred_element_type=f32)
    score_b = jnp.where(causal[None], score_b, 0.0).astype(jnp.bfloat16)
    grad_q = jnp.einsum("hts,shd->thd", score_a, key, preferred_element_type=f32) + jnp.einsum(
        "thb,hab->tha", grad_out, prefix, preferred_element_type=f32
    )
    grad_k = jnp.einsum("htj,thd->jhd", score_a, query, preferred_element_type=f32) + jnp.einsum(
        "jhb,hab->jha", value, suffix, preferred_element_type=f32
    )
    grad_v = jnp.einsum("htj,thd->jhd", score_b, grad_out, preferred_element_type=f32) + jnp.einsum(
        "jha,hab->jhb", key, suffix, preferred_element_type=f32
    )
    joined = jnp.concatenate([grad_q, grad_k, grad_v], axis=1) * scale
    return joined.reshape(count, -1).astype(jnp.bfloat16)


def on_device_any(inputs, queries, keys, values, out_grad):
    tokens = queries.shape[1]
    seq_count = lax.axis_size("seq")
    batch_count = lax.axis_size("dp")
    length_all = tokens * seq_count
    scale = 1.0 / jnp.sqrt(jnp.float32(HS * length_all))
    weight_scale = 1.0 / jnp.sqrt(jnp.float32(batch_count * length_all))
    shape = (tokens, HEADS, HS)
    query = queries[0].reshape(shape)
    key = keys[0].reshape(shape)
    value = values[0].reshape(shape)
    grad_out = out_grad[0].reshape(shape)
    kv_state = jnp.einsum("lhi,lhj->hij", key, value, preferred_element_type=jnp.float32).astype(
        jnp.bfloat16
    )
    dq_state = jnp.einsum(
        "lhi,lhj->hij", query, grad_out, preferred_element_type=jnp.float32
    ).astype(jnp.bfloat16)
    stacked = jnp.stack([kv_state, dq_state])[None]
    position = lax.axis_index("seq")
    piece = lax.all_gather(stacked, "seq", axis=0, tiled=True)
    owners = jnp.arange(piece.shape[0])
    lower = (owners < position).astype(jnp.float32)
    higher = (owners > position).astype(jnp.float32)
    wide = piece.astype(jnp.float32)
    prefix = jnp.einsum("n,nhij->hij", lower, wide[:, 0])
    suffix = jnp.einsum("n,nhij->hij", higher, wide[:, 1])
    prefix = prefix.astype(jnp.bfloat16)
    suffix = suffix.astype(jnp.bfloat16)
    grads = block_grads(query, key, value, grad_out, prefix, suffix, scale)
    features = inputs[0]
    rows_here = lax.psum_scatter(
        (
            lax.dot_general(
                features, grads, (((0,), (0,)), ((), ())), preferred_element_type=jnp.float32
            )
            * weight_scale
        ).astype(jnp.bfloat16),
        "dp",
        scatter_dimension=0,
        tiled=True,
    )
    weight_grad = lax.psum(rows_here, "seq").astype(jnp.float32)
    return (grads[None], weight_grad)


def dot(a, b, a_dim=1, b_dim=0):
    return lax.dot_general(a, b, (((a_dim,), (b_dim,)), ((), ())), preferred_element_type=F32)


def cols(h):
    return slice(h * HS, (h + 1) * HS)


def vmem():
    return pl.BlockSpec(memory_space=pltpu.VMEM)


def smem():
    return pl.BlockSpec(memory_space=pltpu.SMEM)


def params(mebibytes):
    return pltpu.CompilerParams(vmem_limit_bytes=mebibytes << 20)


def hbm():
    return pl.BlockSpec(memory_space=pltpu.HBM)


def state_kernel(meta, q, k, v, g, send, held, sems):
    copies = [
        pltpu.make_async_copy(ref, held.at[i], sems.at[i]) for i, ref in enumerate((q, k, v, g))
    ]
    for copy in copies:
        copy.start()
    for copy in copies:
        copy.wait()
    upper = meta[1] == 1
    for h in range(HEADS):
        left = jnp.where(upper, held[0, :, cols(h)], held[1, :, cols(h)])
        right = jnp.where(upper, held[3, :, cols(h)], held[2, :, cols(h)])
        send[h] = dot(left, right, 0, 0).astype(BF16)


def local_kernel(x, mine, other, local, turned, states, x0, sem):
    copy = pltpu.make_async_copy(x, x0, sem)
    copy.start()
    count = mine.shape[1]
    row = lax.broadcasted_iota(jnp.int32, (count, count), 0)
    col = lax.broadcasted_iota(jnp.int32, (count, count), 1)
    causal = row >= col
    causal_turned = row <= col
    for b, (q, k, v, g) in enumerate(tuple(ref.at[i] for i in range(4)) for ref in (mine, other)):
        for h in range(HEADS):
            qh, kh, vh, gh = (ref[:, cols(h)] for ref in (q, k, v, g))
            qt, kt, vt, gt = qh.T, kh.T, vh.T, gh.T
            a_turned = jnp.where(causal_turned, dot(vh, gt), 0.0).astype(BF16)
            a = jnp.where(causal, dot(gh, vt), 0.0).astype(BF16)
            s = jnp.where(causal, dot(qh, kt), 0.0).astype(BF16)
            local[b, 0, cols(h)] = dot(kt, a_turned)
            local[b, 1, cols(h)] = dot(qt, a)
            local[b, 2, cols(h)] = dot(gt, s)
            states[b, 0, h] = dot(kt, vh).astype(BF16)
            states[b, 1, h] = dot(qt, gh).astype(BF16)
            turned[b, 0, h] = gt
            turned[b, 1, h] = vt
            turned[b, 2, h] = kt
    copy.wait()


def column(table, i):
    return pl.ds(pl.multiple_of(table[4 + i] * BLOCK, BLOCK), BLOCK)


def weights(table, first, grads, x0, x1, out):
    for i in range(0, 8, 2):
        x = jnp.concatenate(
            [
                jnp.concatenate([ref[:, column(table, first + i + j)] for j in range(2)], axis=1)
                for ref in (x0, x1)
            ],
            axis=0,
        )
        total = dot(grads, x)
        out[i] = total[:, :BLOCK].astype(BF16)
        out[i + 1] = total[:, BLOCK:].astype(BF16)


def first_kernel(meta, local, turned, states, near, far, x0, x1, grads, out, *, scale):
    core = meta[0].astype(F32)
    upper = meta[1].astype(F32)
    width = HEADS * HS
    tokens = x0.shape[0]
    for h in range(HEADS):
        outside = near[h].astype(F32) + far[h].astype(F32)
        before = outside * upper
        after = outside * (1.0 - upper)
        for b in range(2):
            late = core if b == 0 else 1.0 - core
            prefix = (before + states[1 - b, 0, h].astype(F32) * late).astype(BF16)
            suffix = (after + states[1 - b, 1, h].astype(F32) * (1.0 - late)).astype(BF16)
            extra = (
                dot(prefix, turned[b, 0, h]),
                dot(suffix, turned[b, 1, h]),
                dot(suffix, turned[b, 2, h], 0, 0),
            )
            for part in range(3):
                total = (local[b, part, cols(h)] + extra[part]) * scale
                rows = slice(part * width + h * HS, part * width + (h + 1) * HS)
                grads[rows, b * tokens : (b + 1) * tokens] = total.astype(BF16)
    weights(meta, 8, grads[:width], x0, x1, out)


def other_kernel(meta, grads, x0, x1, out, *, part):
    width = HEADS * HS
    weights(meta, 16 * part + 8, grads[part * width : (part + 1) * width], x0, x1, out)


def keep_kernel(meta, grads, x0, x1, out_0, out_1, out_2, own):
    width = HEADS * HS
    for part, out in enumerate((out_0, out_1, out_2)):
        weights(meta, 16 * part, grads[part * width : (part + 1) * width], x0, x1, out)
    for i in range(0, grads.shape[0], HS):
        own[:, i : i + HS] = grads[i : i + HS, : own.shape[0]].T


def place_kernel(meta, *refs, parts, first):
    out, wide, sems = refs[-3:]
    copies = []
    size = wide.shape[3]
    for part in range(parts):
        columns = pl.ds((first + part) * size, size)
        for i, (turn, block) in enumerate(zip((0, 2, 1, 3), refs[4 * part : 4 * part + 4])):
            wide[part, i] = block[...].astype(F32)
            rows = pl.ds(pl.multiple_of((meta[2] ^ turn) * BLOCK, BLOCK), BLOCK)
            copy = pltpu.make_async_copy(wide.at[part, i], out.at[rows, columns], sems.at[part, i])
            copy.start()
            copies.append(copy)
    for copy in copies:
        copy.wait()


def place(meta, blocks, first, shape, before=()):
    parts = len(blocks) // 4
    return pl.pallas_call(
        functools.partial(place_kernel, parts=parts, first=first),
        in_specs=[smem()] + [vmem()] * len(blocks) + [hbm()] * len(before),
        out_specs=hbm(),
        out_shape=jax.ShapeDtypeStruct(shape, F32),
        scratch_shapes=[
            pltpu.VMEM((parts, 4, *blocks[0].shape), F32),
            pltpu.SemaphoreType.DMA((parts, 4)),
        ],
        input_output_aliases={len(blocks) + 1: 0} if before else {},
        compiler_params=params(8),
    )(meta, *blocks, *before)


def final_kernel(total, here, out, *, scale):
    out[...] = ((total[0] + here[0].astype(F32)) * scale).T.astype(BF16)


def after(value, *others):
    return lax.optimization_barrier((value, *others))[0]


def partners(core0, core1, seq_count, dp_count):
    pairs = []
    for s in range(seq_count):
        for d in range(dp_count):
            ds, dd = (core0, core1)[s % 2]
            pairs.append((s * dp_count + d, (s ^ ds) * dp_count + (d ^ dd)))
    return pairs


def on_device(inputs, queries, keys, values, out_grad):
    tokens = queries.shape[1]
    seq_count = lax.axis_size("seq")
    dp_count = lax.axis_size("dp")
    length_all = tokens * seq_count
    scale = float(1.0 / (HS * length_all) ** 0.5)
    weight_scale = float(1.0 / (dp_count * length_all) ** 0.5)
    features = inputs[0]
    blocks = [value[0] for value in (queries, keys, values, out_grad)]
    stay = lambda value: pltpu.with_memory_space_constraint(value, pltpu.HBM)
    width = blocks[0].shape[1]
    rows = features.shape[1] // (seq_count * dp_count)

    swap = lambda value, core0, core1: lax.ppermute(
        value, AXES, partners(core0, core1, seq_count, dp_count)
    )
    sibling, across, y, z1, z2 = (1, 0), (2, 0), (0, 1), (0, 2), (0, 4)

    s, d = lax.axis_index("seq"), lax.axis_index("dp")
    core, upper = s & 1, s >> 1
    orders = (
        ((across, y), (y, z1), (z1, across), (z2, z2)),
        ((across, y), (y, across), (z1, z1), (z2, z2)),
        ((z1, z1), (y, across), (across, y), (z2, z2)),
    )
    lane = jnp.arange(4 + 16 * len(orders), dtype=jnp.int32)
    bits = lane - 4
    spot = jnp.zeros_like(lane)
    for part, order in enumerate(orders):
        for i, way in enumerate(order):
            bit = (bits >> (3 - i)) & 1
            jump = [ds | dd * seq_count for ds, dd in way]
            flip = bit * jnp.where(core == 0, jump[0], jump[1])
            spot = spot ^ jnp.where(bits >> 4 == part, flip, 0)
    spot = spot ^ (d * seq_count + s)
    meta = jnp.where(
        lane == 0, core, jnp.where(lane == 1, upper, jnp.where(lane == 2, s, spot))
    ).astype(jnp.int32)

    send, mine = pl.pallas_call(
        state_kernel,
        in_specs=[smem()] + [hbm()] * 4,
        out_specs=[vmem()] * 2,
        out_shape=[
            jax.ShapeDtypeStruct((HEADS, HS, HS), BF16),
            jax.ShapeDtypeStruct((4, tokens, width), BF16),
        ],
        scratch_shapes=[pltpu.SemaphoreType.DMA((4,))],
        compiler_params=params(4),
    )(meta, *map(stay, blocks))
    near = swap(send, across, across)
    other = swap(mine, sibling, sibling)
    other_x = swap(features, sibling, sibling)

    local, turned, states, mine_x = pl.pallas_call(
        local_kernel,
        in_specs=[hbm()] + [vmem()] * 2,
        out_specs=[vmem()] * 4,
        out_shape=[
            jax.ShapeDtypeStruct((2, 3, width, tokens), F32),
            jax.ShapeDtypeStruct((2, 3, HEADS, HS, tokens), BF16),
            jax.ShapeDtypeStruct((2, 2, HEADS, HS, HS), BF16),
            jax.ShapeDtypeStruct(features.shape, BF16),
        ],
        scratch_shapes=[pltpu.SemaphoreType.DMA],
        compiler_params=params(16),
    )(stay(features), mine, other)
    near = after(near, states)
    far = swap(near, sibling, sibling)
    half = jax.ShapeDtypeStruct((8, width, BLOCK), BF16)
    grads, going = pl.pallas_call(
        functools.partial(first_kernel, scale=scale),
        in_specs=[smem()] + [vmem()] * 7,
        out_specs=[vmem()] * 2,
        out_shape=[jax.ShapeDtypeStruct((3 * width, 2 * tokens), BF16), half],
        compiler_params=params(16),
    )(meta, local, turned, states, near, far, mine_x, other_x)
    here = [swap(going, *orders[0][0]), None, None]
    for part in (2, 1):
        going = pl.pallas_call(
            functools.partial(other_kernel, part=part),
            in_specs=[smem()] + [vmem()] * 3,
            out_specs=vmem(),
            out_shape=half,
            compiler_params=params(16),
        )(meta, after(grads, going), mine_x, other_x)
        here[part] = swap(going, *orders[part][0])
    *kept, own = pl.pallas_call(
        keep_kernel,
        in_specs=[smem()] + [vmem()] * 3,
        out_specs=[vmem()] * 4,
        out_shape=[half] * 3 + [jax.ShapeDtypeStruct((tokens, 3 * width), BF16)],
        compiler_params=params(16),
    )(meta, after(grads, going), mine_x, other_x)

    def step(kept, here, way):
        count = kept.shape[0] // 2
        total = kept.astype(F32) + here.astype(F32)
        going = total[count:].astype(BF16)
        return total[:count], going, swap(going, *way)

    def finish(kept, here):
        final = pl.pallas_call(
            functools.partial(final_kernel, scale=weight_scale),
            in_specs=[vmem()] * 2,
            out_specs=vmem(),
            out_shape=jax.ShapeDtypeStruct((BLOCK, kept.shape[1]), BF16),
            compiler_params=params(4),
        )(kept, here)
        facing = swap(final, across, across)
        return final, facing, swap(final, sibling, sibling), swap(facing, sibling, sibling)

    latest = kept[0]
    for part, level in ((0, 1), (1, 1), (2, 1), (0, 2), (1, 2), (2, 2), (0, 3), (2, 3), (1, 3)):
        kept[part], latest, here[part] = step(
            kept[part], after(here[part], latest), orders[part][level]
        )
    parts = {}
    parts[0] = finish(kept[0], after(here[0], latest))
    parts[2] = finish(kept[2], after(here[2], parts[0][0]))
    parts[1] = finish(kept[1], after(here[1], parts[2][0], parts[0][1]))
    shape = (seq_count * rows, 3 * width)
    weight_grad = place(meta, parts[0] + parts[1] + parts[2], 0, shape)
    return (own[None], weight_grad)


def solution(mesh):
    in_specs = (
        P("dp", "seq", None),
        P("dp", "seq", None),
        P("dp", "seq", None),
        P("dp", "seq", None),
        P("dp", "seq", None),
    )
    out_specs = (P("dp", "seq", None), P("dp", None))
    fast = mesh.shape["seq"] == 4 and mesh.shape["dp"] == 8
    body = on_device if fast else on_device_any
    return jax.shard_map(
        body, mesh=mesh, in_specs=in_specs, out_specs=out_specs, check_vma=False
    )
```
